128 devices in a mesh: gx: 16 (over z, x_hi, core), gy: 8 (over x_lo, y).
Axes of the slice: x: 4 (x_hi: 2, x_lo: 2; x = x_hi * 2 + x_lo), y: 4, z: 4, core: 2. Of those that a mesh axis runs over, the one named last changes fastest.
Arguments:
- atom_cell: int32 [3, 16, 16, 128, 576], P(None, 'gx', 'gy'), may hold values from 0 to 7
- atom_frac: float32 [3, 16, 16, 128, 576], P(None, 'gx', 'gy'), may hold values from 0 to 1
- atom_weight: float32 [16, 16, 128, 576], P('gx', 'gy'), may hold values from 0.5 to 1.5
- block_count: int32 [16, 16, 128], P('gx', 'gy'), may hold values from 384 to 576, as said below
- miller_h: int32 [8], replicated, may hold values from 9 to 25
- miller_k: int32 [8], replicated, may hold values from 9 to 25
- miller_l: int32 [8], replicated, may hold values from 9 to 204
Outputs:
- density: float32 [128, 128, 1024], P('gx', 'gy')
- intensity: float32 [128, 256], P(('gx', 'gy'))
The draws below stay inside these ranges and needn't reach their ends.
Inputs may be any that keep to these rules, and one draw needn't show every extreme that they name: `block_count`: slots 0 to count - 1 of a block hold its atoms; every device holds a block with exactly 576 atoms.
All inputs are finite; a program needn't handle non-finite values.
Results may differ from the reference program's by a relative error of at most 0.0023.
Values sent between devices are 32-bit elements; how exact they have to be, the bound alone decides.
A program may use at most 192 MiB of HBM per device.

```python
import math
import jax
import jax.numpy as jnp
from jax import lax

CX = 8
CY = 16
CZ = 1024
CAP = 576
WINDOWS = 8
NX = 128
NY = 128


def draw_block_count(key, part):
    extent = (NX // 8, NY // 8, CZ // 8)
    counts = jax.random.randint(key, extent, CAP * 2 // 3, CAP + 1, dtype=jnp.int32)
    per_x = CX // 8
    per_y = CY // 8
    chosen = jax.random.randint(jax.random.fold_in(key, 7), (NX // CX, NY // CY), 0, CZ // 8, dtype=jnp.int32)
    owner_x = jnp.arange(NX // 8, dtype=jnp.int32) // per_x
    owner_y = jnp.arange(NY // 8, dtype=jnp.int32) // per_y
    target = chosen[owner_x][:, owner_y]
    corner_block = (jnp.arange(NX // 8) % per_x == 0)[:, None] & (jnp.arange(NY // 8) % per_y == 0)[None, :]
    forced = corner_block[:, :, None] & (jnp.arange(CZ // 8, dtype=jnp.int32)[None, None, :] == target[:, :, None])
    return jnp.where(forced, jnp.full(extent, CAP, jnp.int32), counts)


def touch_ends(values, key, low, high):
    longest = values.shape.index(max(values.shape))
    spots = []
    for shift in (0, 1):
        where = [jax.random.randint(jax.random.fold_in(key, axis), (), 0, length) for axis, length in enumerate(values.shape)]
        where[longest] = (where[longest] + shift) % values.shape[longest]
        spots.append(tuple(where))
    return values.at[spots[0]].set(low).at[spots[1]].set(high)


def levels(stream_key, shape, split, least, largest):
    loudness = 1.0
    for dim, blocks in split:
        steps = jax.random.uniform(jax.random.fold_in(jax.random.fold_in(stream_key, 6), dim), (blocks,), jnp.float32, least / len(split), largest / len(split))
        loudness = loudness * jnp.repeat(jnp.exp(steps), shape[dim] // blocks).reshape((-1,) + (1,) * (len(shape) - 1 - dim))
    return loudness


def setup_inputs(seed: int = 0) -> dict:
    streams_of = jax.random.split(jax.random.key(seed), 8)
    atom_cell = touch_ends(jax.random.randint(streams_of[0], (3, NX // 8, NY // 8, CZ // 8, CAP), 0, 8), jax.random.fold_in(streams_of[0], 1), 0, 7).astype(jnp.int32)
    atom_frac = jnp.clip(1.0 * jax.random.uniform(streams_of[1], (3, NX // 8, NY // 8, CZ // 8, CAP), jnp.float32) ** levels(streams_of[1], (3, NX // 8, NY // 8, CZ // 8, CAP), ((1, 16), (2, 8)), -0.2, 0.2), 0.0, 1.0)
    atom_weight = jnp.clip(0.5 + 1.0 * jax.random.uniform(streams_of[2], (NX // 8, NY // 8, CZ // 8, CAP), jnp.float32) ** levels(streams_of[2], (NX // 8, NY // 8, CZ // 8, CAP), ((0, 16), (1, 8)), -0.2, 0.2), 0.5, 1.5)
    block_count = draw_block_count(jax.random.fold_in(streams_of[7], 71), 0)
    miller_h = touch_ends(jax.random.randint(streams_of[4], (WINDOWS,), 9, NX // 5 + 1), jax.random.fold_in(streams_of[4], 1), 9, (NX // 5 + 1) - 1).astype(jnp.int32)
    miller_k = touch_ends(jax.random.randint(streams_of[5], (WINDOWS,), 9, NY // 5 + 1), jax.random.fold_in(streams_of[5], 1), 9, (NY // 5 + 1) - 1).astype(jnp.int32)
    miller_l = touch_ends(jax.random.randint(streams_of[6], (WINDOWS,), 9, CZ // 5 + 1), jax.random.fold_in(streams_of[6], 1), 9, (CZ // 5 + 1) - 1).astype(jnp.int32)
    return dict(atom_cell=atom_cell, atom_frac=atom_frac, atom_weight=atom_weight, block_count=block_count, miller_h=miller_h, miller_k=miller_k, miller_l=miller_l)


KERNEL_SIGMA = 0.9
NORMAL = 1.0 / (KERNEL_SIGMA * math.sqrt(2.0 * math.pi))
EXACT_DOT = lax.Precision.HIGHEST

def kernel_taps(offsets, fraction):
    tap_rows = jnp.arange(16, dtype=jnp.int32)
    differ = tap_rows - offsets[..., None]
    inside = (differ >= 1) & (differ <= 8)
    distance = (differ - 4).astype(jnp.float32) - fraction[..., None]
    values = jnp.exp(distance * distance * (-0.5 / (KERNEL_SIGMA * KERNEL_SIGMA))) * NORMAL
    return jnp.where(inside, values, jnp.zeros_like(values))

def to_bfloat(values):
    return lax.optimization_barrier(values.astype(jnp.bfloat16)).astype(jnp.float32)

def footprints(offsets, fraction, weights, counts):
    blocks, capacity = weights.shape
    slot_ids = jnp.arange(capacity, dtype=jnp.int32)
    occupied = (slot_ids[None, :] < counts[:, None]).astype(jnp.float32)
    taps_x = kernel_taps(offsets[0], fraction[0])
    taps_y = kernel_taps(offsets[1], fraction[1])
    taps_z = kernel_taps(offsets[2], fraction[2])
    scaled = to_bfloat((weights * occupied)[..., None] * taps_z)
    crossed = to_bfloat((taps_x[..., :, None] * taps_y[..., None, :]).reshape(blocks, capacity, 256))
    return jnp.einsum('bpc,bpm->bcm', scaled, crossed, precision=EXACT_DOT)

def pad_along(values, along, leading, trailing):
    widths = [(0, 0)] * values.ndim
    widths[along] = (leading, trailing)
    return jnp.pad(values, widths)

def wrap_fold(padded, along, length):
    interior = lax.slice_in_dim(padded, 4, length + 4, axis=along)
    leading = lax.slice_in_dim(padded, 0, 4, axis=along)
    trailing = lax.slice_in_dim(padded, length + 4, length + 8, axis=along)
    return interior + pad_along(trailing, along, 0, length - 4) + pad_along(leading, along, length - 4, 0)

def z_column(foot, depth_cells):
    nblocks = foot.shape[0]
    halves = foot.reshape(nblocks, 2, 8, 256)
    lower_half = pad_along(halves[:, 0], 0, 0, 1)
    upper_half = pad_along(halves[:, 1], 0, 1, 0)
    joined = (lower_half + upper_half).reshape((nblocks + 1) * 8, 256)
    folded = wrap_fold(joined, 0, depth_cells)
    return jnp.transpose(folded, (1, 0)).reshape(16, 16, depth_cells)

def phases(freqs, positions, extent):
    shifted = freqs[:, None] + jnp.arange(16, dtype=jnp.int32)[None, :] - 8
    product = positions[:, None, None] * shifted[None, :, :] % extent
    angles = product.astype(jnp.float32) * (2.0 * math.pi / extent)
    return (jnp.cos(angles), jnp.sin(angles))

def reference(atom_cell, atom_frac, atom_weight, block_count, miller_h, miller_k, miller_l):
    blocks_x, blocks_y, blocks_z, capacity = atom_weight.shape
    columns_total = blocks_x * blocks_y
    offsets = atom_cell.reshape(3, columns_total, blocks_z, capacity)
    fraction = atom_frac.reshape(3, columns_total, blocks_z, capacity)
    weights = atom_weight.reshape(columns_total, blocks_z, capacity)
    counts = block_count.reshape(columns_total, blocks_z)

    def deposit(padded_grid, column_index):
        foot = footprints(offsets[:, column_index], fraction[:, column_index], weights[column_index], counts[column_index])
        column = z_column(foot, CZ)
        start_x = (column_index // blocks_y * 8).astype(jnp.int32)
        start_y = (column_index % blocks_y * 8).astype(jnp.int32)
        anchor = jnp.zeros((), jnp.int32)
        current = lax.dynamic_slice(padded_grid, (start_x, start_y, anchor), (16, 16, CZ))
        return (lax.dynamic_update_slice(padded_grid, current + column, (start_x, start_y, anchor)), None)
    empty_grid = jnp.zeros((NX + 8, NY + 8, CZ), jnp.float32)
    padded_grid = lax.scan(deposit, empty_grid, jnp.arange(columns_total, dtype=jnp.int32))[0]
    density = wrap_fold(wrap_fold(padded_grid, 0, NX), 1, NY)
    windows = miller_h.shape[0]
    cos_z, sin_z = phases(miller_l, jnp.arange(CZ, dtype=jnp.int32), CZ)
    table_z = jnp.concatenate([cos_z, -sin_z], axis=1).reshape(CZ, 2 * windows * 16)
    partial_value = jnp.dot(density.reshape(NX * NY, CZ), table_z, precision=EXACT_DOT, preferred_element_type=jnp.float32)
    partial_value = partial_value.reshape(NX, NY, 2, windows, 16)
    part_real = partial_value[:, :, 0]
    part_imag = partial_value[:, :, 1]
    cos_y, sin_y = phases(miller_k, jnp.arange(NY, dtype=jnp.int32), NY)
    half_real = jnp.einsum('xywl,ywk->wxkl', part_real, cos_y, precision=EXACT_DOT) + jnp.einsum('xywl,ywk->wxkl', part_imag, sin_y, precision=EXACT_DOT)
    half_imag = jnp.einsum('xywl,ywk->wxkl', part_imag, cos_y, precision=EXACT_DOT) - jnp.einsum('xywl,ywk->wxkl', part_real, sin_y, precision=EXACT_DOT)
    cos_x, sin_x = phases(miller_h, jnp.arange(NX, dtype=jnp.int32), NX)
    wave_real = jnp.einsum('xwh,wxkl->whkl', cos_x, half_real, precision=EXACT_DOT) + jnp.einsum('xwh,wxkl->whkl', sin_x, half_imag, precision=EXACT_DOT)
    wave_imag = jnp.einsum('xwh,wxkl->whkl', cos_x, half_imag, precision=EXACT_DOT) - jnp.einsum('xwh,wxkl->whkl', sin_x, half_real, precision=EXACT_DOT)
    intensity = (wave_real * wave_real + wave_imag * wave_imag) / float(NX * NY * CZ)
    return (density, intensity.reshape(windows * 16, 256))
```

```python
import math
import jax, jax.numpy as jnp
from jax import lax
from jax.experimental import pallas as pl
from jax.experimental.pallas import tpu as pltpu
from jax.sharding import PartitionSpec as P

SIGMA2 = 0.9 * 0.9
INV = 1.0 / SIGMA2
NORMAL = 1.0 / (0.9 * math.sqrt(2.0 * math.pi))
F32 = jnp.float32
BF16 = jnp.bfloat16
NT = (((1,), (1,)), ((), ()))
NN = (((1,), (0,)), ((), ()))


def iota(shape, dim):
    return lax.broadcasted_iota(jnp.int32, shape, dim)


def slot(row):
    return row - 4 if row >= 4 else row + 12


def dense_taps(cell, frac, scale, out, buf, tile):
    u = cell.astype(F32) + (frac - 4.0)
    up = jnp.exp(u * INV)
    down = jnp.exp(u * (-INV))
    mid = jnp.exp(u * u * (-0.5 * INV)) * scale
    out[buf, tile, 32:40, :] = mid
    for sign, ratio in ((1, up), (-1, down)):
        p = mid
        for k in range(1, 8):
            p = p * (ratio * math.exp(-(2 * k - 1) * 0.5 * INV))
            r = slot(8 + sign * k)
            keep = cell >= k if sign > 0 else cell <= 7 - k
            out[buf, tile, 8 * r : 8 * r + 8, :] = jnp.where(keep, p, 0.0)


def crossed(x, y, buf, tile, b):
    yy = y[buf, tile, pl.ds(b, 16, stride=8), :].astype(BF16)
    parts = []
    for a in range(16):
        if a == 12:
            parts.append(jnp.zeros((16, 128), BF16))
            continue
        x8 = x[buf, tile, pl.ds(a * 8 + b, 8, stride=0), :]
        parts.append(jnp.concatenate([x8, x8], 0).astype(BF16) * yy)
    return jnp.concatenate(parts, 0)


def sincos(q, extent):
    eighth = extent // 8
    s = q + eighth
    quad = (s >> (extent.bit_length() - 3)) & 3
    r = ((s & (2 * eighth - 1)) - eighth).astype(F32) * (2.0 * math.pi / extent)
    r2 = r * r
    sin = r * (1.0 + r2 * (-1 / 6 + r2 * (1 / 120 + r2 * (-1 / 5040 + r2 * (1 / 362880)))))
    cos = 1.0 + r2 * (-0.5 + r2 * (1 / 24 + r2 * (-1 / 720 + r2 * (1 / 40320 + r2 * (-1 / 3628800)))))
    odd = (quad & 1) == 1
    c = jnp.where(odd, sin, cos)
    s = jnp.where(odd, cos, sin)
    c = jnp.where((quad == 1) | (quad == 2), -c, c)
    s = jnp.where(quad >= 2, -s, s)
    return c, s


def split(v):
    hi = v.astype(BF16)
    return hi, (v - hi.astype(F32)).astype(BF16)


def mm(a, b, dims=NN):
    return lax.dot_general(a, b, dims, preferred_element_type=F32)


def local_kernel(
    cnt, cell, frac, w, mh, mk, ml,
    y_out, up_out, down_out, r_out,
    packed, fx, fy, fz, ws, xs, ys, zs, inner, edge, tab_hi, tab_lo, zsum, tt, d_hi, d_lo,
):
    def pieces(fn, out):
        for t in range(9):
            if t < 8:
                v = fn(t // 4, 128 * (t % 4), 128)
            else:
                v = jnp.concatenate([fn(0, 512, 64), fn(1, 512, 64)], 0)
            out[t] = v.T

    pieces(lambda c, s, n: cell[0, c, s : s + n] + cell[1, c, s : s + n] * 8 + cell[2, c, s : s + n] * 64, packed)
    for d, o in ((0, fx), (1, fy), (2, fz)):
        pieces(lambda c, s, n: frac[d, c, s : s + n], o)

    def weigh(c, s, n):
        return jnp.where(iota((n, 128), 0) + s < cnt[c : c + 1, :], w[c, s : s + n] * NORMAL, 0.0)

    pieces(weigh, ws)
    for o in (ys, zs):
        for buf in range(2):
            for t in range(9):
                o[buf, t, 96:104, :] = jnp.zeros((8, 128), F32)

    def dense(g, buf):
        gs = pl.ds(pl.multiple_of(g * 8, 8), 8)
        for t in range(9):
            q = packed[t, gs, :]
            dense_taps(q & 7, fx[t, gs, :], NORMAL, xs, buf, t)
            dense_taps((q >> 3) & 7, fy[t, gs, :], NORMAL, ys, buf, t)
            dense_taps(q >> 6, fz[t, gs, :], ws[t, gs, :], zs, buf, t)

    dense(0, 0)
    lane16 = iota((16, 128), 1)

    def group(g, _):
        buf = g & 1
        for b in range(8):
            zt = zs[buf, 8, pl.ds(b, 16, stride=8), :]
            zm = jnp.concatenate([jnp.where(lane16 < 64, zt, 0.0), jnp.where(lane16 < 64, 0.0, zt)], 0).astype(BF16)
            fm = mm(zm, crossed(xs, ys, buf, 8, b), NT)
            for c in range(2):
                f = fm[16 * c : 16 * c + 16]
                for t in (4 * c, 4 * c + 2):
                    zz = jnp.concatenate([zs[buf, t + e, pl.ds(b, 16, stride=8), :] for e in (0, 1)], 1).astype(BF16)
                    cc = jnp.concatenate([crossed(xs, ys, buf, t + e, b) for e in (0, 1)], 1)
                    f = f + mm(zz, cc, NT)
                base = pl.multiple_of(g * 64 + b * 8, 8)
                inner[c, pl.ds(base, 8), :] = f[0:8]
                edge[c, pl.ds(base + 8, 8), :] = f[8:16]
        dense(jnp.minimum(g + 1, 15), 1 - buf)
        return 0

    lax.fori_loop(0, 16, group, 0)
    for c in range(2):
        edge[c, 0:8, :] = edge[c, 1024:1032, :]
        edge[c, 1032:1040, :] = edge[c, 8:16, :]

    row8 = iota((8, 128), 0)
    lane8 = iota((8, 128), 1)
    ls = [ml[v // 2] + (row8 + 8 * (v % 2) - 8) for v in range(16)]
    lcol = jnp.concatenate(ls, 0)
    zl = iota((128, 128), 1)
    c0, s0 = sincos((lcol * zl) & 1023, 1024)
    cw, sw = sincos((lcol * 128) & 1023, 1024)
    for t in range(8):
        for half, v in ((0, c0), (1, -s0)):
            hi, lo = split(v)
            tab_hi[128 * half : 128 * half + 128, 128 * t : 128 * t + 128] = hi
            tab_lo[128 * half : 128 * half + 128, 128 * t : 128 * t + 128] = lo
        c0, s0 = c0 * cw - s0 * sw, s0 * cw + c0 * sw

    low256 = (iota((256, 256), 0) & 7) < 4
    for c in range(2):
        def ztile(t, _, c=c):
            zs0 = pl.multiple_of(t * 256, 256)
            d = inner[c, pl.ds(zs0, 256), :] + jnp.where(
                low256, edge[c, pl.ds(zs0, 256), :], edge[c, pl.ds(zs0 + 16, 256), :]
            )
            tt[c, :, pl.ds(zs0, 256)] = d.T
            hi, lo = split(d)
            d_hi[...] = hi
            d_lo[...] = lo
            th = tab_hi[:, pl.ds(zs0, 256)]
            tl = tab_lo[:, pl.ds(zs0, 256)]
            part = mm(th, d_hi[...]) + mm(th, d_lo[...]) + mm(tl, d_hi[...])

            @pl.when(t == 0)
            def _():
                zsum[c] = part

            @pl.when(t > 0)
            def _():
                zsum[c] += part

            return 0

        lax.fori_loop(0, 4, ztile, 0)

    low = iota((8, 1024), 0) < 4
    for k in range(8):
        tops, bottoms = [], []
        for a in (2 * k, 2 * k + 1):
            in0, out0 = tt[0, 16 * a : 16 * a + 8, :], tt[0, 16 * a + 8 : 16 * a + 16, :]
            in1, out1 = tt[1, 16 * a : 16 * a + 8, :], tt[1, 16 * a + 8 : 16 * a + 16, :]
            y_out[a, 0:8, :] = in0 + jnp.where(low, 0.0, out1)
            y_out[a, 8:16, :] = in1 + jnp.where(low, out0, 0.0)
            tops.append(out1)
            bottoms.append(out0)
        up_out[k] = jnp.where(low, tops[0], pltpu.roll(tops[1], 4, 0))
        down_out[k] = jnp.where(low, pltpu.roll(bottoms[0], 4, 0), bottoms[1])

    x0 = lax.axis_index("gx") * 8
    y0 = lax.axis_index("gy") * 16
    n = iota((16, 256), 1)
    ip = (n & 63) >> 2
    ni = (ip & 1) * 8 + (ip >> 1) - 8
    nj = (n >> 6) * 4 + (n & 3) - 8
    off = iota((16, 256), 0)
    off = jnp.where(off < 12, off, off - 16)
    lane_low = iota((16, 128), 1) < 64

    def pair(v, _):
        us = []
        for e in range(2):
            win = 2 * v + e
            hx = mh[win] + ni
            ky = mk[win] + nj
            xr, xi = sincos((hx * (x0 + off)) & 127, 128)
            yr, yi = sincos((ky * (y0 + off)) & 127, 128)
            pr, pi = sincos((ky[0:1] * 8) & 127, 128)
            mr, mi = [], []
            for a in range(16):
                mr.append(xr[a : a + 1] * yr - xi[a : a + 1] * yi)
                mi.append(-(xr[a : a + 1] * yi + xi[a : a + 1] * yr))
            mr = jnp.concatenate(mr, 0)
            mi = jnp.concatenate(mi, 0)
            mrh, mrl = split(mr)
            mih, mil = split(mi)
            rows = [
                zsum[c, pl.ds(pl.multiple_of(128 * half + win * 16, 16), 16), :] for c in (0, 1) for half in (0, 1)
            ]
            zh, zl_ = split(jnp.concatenate(rows, 0))
            A = mm(zh, mrh) + mm(zl_, mrh) + mm(zh, mrl)
            B = mm(zh, mih) + mm(zl_, mih) + mm(zh, mil)
            re0, im0 = A[0:16] - B[16:32], A[16:32] + B[0:16]
            re1, im1 = A[32:48] - B[48:64], A[48:64] + B[32:48]
            re = re0 + re1 * pr + im1 * pi
            im = im0 + im1 * pr - re1 * pi
            us.append((re, im))
        rows = []
        for jh in range(4):
            for part in range(2):
                a0 = us[0][part][:, 128 * (jh // 2) : 128 * (jh // 2) + 128]
                a1 = us[1][part][:, 128 * (jh // 2) : 128 * (jh // 2) + 128]
                if jh % 2 == 0:
                    rows.append(jnp.where(lane_low, a0, pltpu.roll(a1, 64, 1)))
                else:
                    rows.append(jnp.where(lane_low, pltpu.roll(a0, 64, 1), a1))
        tr = jnp.concatenate(rows, 0).T
        for e in range(2):
            for il in range(8):
                r_out[il, 2 * v + e] = tr[64 * e + 8 * il : 64 * e + 8 * il + 8]
        return 0

    lax.fori_loop(0, 4, pair, 0)


def local(cell, frac, w, cnt, mh, mk, ml):
    cell = jnp.swapaxes(cell, 2, 3)
    frac = jnp.swapaxes(frac, 2, 3)
    w = jnp.swapaxes(w, 1, 2)
    vm = pl.BlockSpec(memory_space=pltpu.VMEM)
    sm = pl.BlockSpec(memory_space=pltpu.SMEM)
    sd = jax.ShapeDtypeStruct
    return pl.pallas_call(
        local_kernel,
        out_shape=(sd((16, 16, 1024), F32), sd((8, 8, 1024), F32), sd((8, 8, 1024), F32), sd((8, 8, 8, 128), F32)),
        in_specs=[vm] * 4 + [sm] * 3,
        out_specs=(vm,) * 4,
        scratch_shapes=[pltpu.VMEM((9, 128, 128), jnp.int32)]
        + [pltpu.VMEM((9, 128, 128), F32)] * 4
        + [pltpu.VMEM((2, 9, 128, 128), F32)] * 3
        + [
            pltpu.VMEM((2, 1024, 256), F32),
            pltpu.VMEM((2, 1040, 256), F32),
            pltpu.VMEM((256, 1024), BF16),
            pltpu.VMEM((256, 1024), BF16),
            pltpu.VMEM((2, 256, 256), F32),
            pltpu.VMEM((2, 256, 1024), F32),
            pltpu.VMEM((256, 256), BF16),
            pltpu.VMEM((256, 256), BF16),
        ],
        compiler_params=pltpu.CompilerParams(vmem_limit_bytes=60 * 2**20),
    )(cnt, cell, frac, w, mh, mk, ml)


MESH = pl.DeviceIdType.MESH
CHUNK = 256


def exchange_kernel(
    y_in, up_in, down_in, r_in, dens, inten,
    q, up_got, down_got, left_got, right_got, got1, part, got2,
    s1, g1, s2, g2, up_s, up_g, down_s, down_g, right_s, right_g, left_s, left_g,
):
    nx, ny = lax.axis_size("gx"), lax.axis_size("gy")
    me_x, me_y = lax.axis_index("gx"), lax.axis_index("gy")
    barrier = pltpu.get_barrier_semaphore()

    def greet_y(d, _):
        pl.semaphore_signal(barrier, inc=1, device_id=(me_x, (me_y + d) % ny), device_id_type=MESH)
        return 0

    def greet_x(d, _):
        pl.semaphore_signal(barrier, inc=1, device_id=((me_x + d) % nx, me_y), device_id_type=MESH)
        return 0

    lax.fori_loop(1, ny, greet_y, 0)
    lax.fori_loop(1, nx, greet_x, 0)
    pl.semaphore_wait(barrier, nx + ny - 2)

    def first(d):
        to = (me_y + d) % ny
        return pltpu.make_async_remote_copy(
            r_in.at[to], got1.at[d], s1.at[d], g1.at[d], device_id=(me_x, to), device_id_type=MESH
        )

    def second(d):
        to = (me_x + d) % nx
        return pltpu.make_async_remote_copy(
            part.at[to // 2], got2.at[d], s2.at[d], g2.at[d], device_id=(to, me_y), device_id_type=MESH
        )

    def piece(src, dst, ss, gs, c, to):
        z = pl.ds(c * CHUNK, CHUNK)
        return pltpu.make_async_remote_copy(
            src.at[:, :, z], dst.at[:, :, z], ss.at[c], gs.at[c], device_id=to, device_id_type=MESH
        )

    up = lambda c: piece(up_in, up_got, up_s, up_g, c, (me_x, (me_y + 1) % ny))
    down = lambda c: piece(down_in, down_got, down_s, down_g, c, (me_x, (me_y + ny - 1) % ny))
    right = lambda c: piece(q.at[pl.ds(8, 4)], right_got, right_s, right_g, c, ((me_x + 1) % nx, me_y))
    left = lambda c: piece(q.at[pl.ds(12, 4)], left_got, left_s, left_g, c, ((me_x + nx - 1) % nx, me_y))

    def start(copy):
        def body(i, _):
            copy(i).start()
            return 0

        return body

    def finish(copy):
        def body(i, _):
            copy(i).wait()
            return 0

        return body

    lax.fori_loop(1, ny, start(first), 0)
    for c in range(4):
        up(c).start()
        down(c).start()

    low = iota((8, CHUNK), 0) < 4
    for c in range(4):
        z = slice(c * CHUNK, c * CHUNK + CHUNK)
        up(c).wait()
        down(c).wait()
        for k in (4, 5, 6, 7, 0, 1, 2, 3):
            a = 2 * k
            u, d = up_got[k, :, z], down_got[k, :, z]
            q[a, 0:8, z] = y_in[a, 0:8, z] + jnp.where(low, u, 0.0)
            q[a + 1, 0:8, z] = y_in[a + 1, 0:8, z] + jnp.where(low, pltpu.roll(u, 4, 0), 0.0)
            q[a, 8:16, z] = y_in[a, 8:16, z] + jnp.where(low, 0.0, pltpu.roll(d, 4, 0))
            q[a + 1, 8:16, z] = y_in[a + 1, 8:16, z] + jnp.where(low, 0.0, d)
        right(c).start()
        left(c).start()

    lax.fori_loop(1, ny, finish(first), 0)
    part[...] = r_in[me_y] + lax.fori_loop(2, ny, lambda d, t: t + got1[d], got1[1])
    lax.fori_loop(1, nx, start(second), 0)
    lax.fori_loop(1, nx, finish(second), 0)
    total = part[me_x // 2] + lax.fori_loop(2, nx, lambda d, t: t + got2[d], got2[1])
    mine = jnp.where((iota((8, 128), 0) * 0 + me_x % 2) == 1, pltpu.roll(total, 4, 0), total)
    power = mine * mine
    power = power + pltpu.roll(power, 112, 1)
    n = iota((128, 256), 1)
    pick = (iota((128, 256), 0) == (n >> 6) * 32 + (n & 15)).astype(F32)
    wide = lax.dot_general(power, pick, NN, precision=lax.Precision.HIGHEST, preferred_element_type=F32)
    keep = iota((8, 256), 0) == ((iota((8, 256), 1) >> 4) & 3)
    inten[...] = jnp.sum(jnp.where(keep, wide, 0.0), axis=0, keepdims=True) * (1.0 / 16777216.0)

    for c in range(4):
        z = slice(c * CHUNK, c * CHUNK + CHUNK)
        right(c).wait()
        left(c).wait()
        dens[0:4, :, z] = q[0:4, :, z] + right_got[:, :, z]
        dens[4:8, :, z] = q[4:8, :, z] + left_got[:, :, z]


def exchange(y, up, down, r):
    vm = pl.BlockSpec(memory_space=pltpu.VMEM)
    sd = jax.ShapeDtypeStruct
    dma = pltpu.SemaphoreType.DMA
    return pl.pallas_call(
        exchange_kernel,
        out_shape=(sd((8, 16, 1024), F32), sd((1, 256), F32)),
        in_specs=[vm] * 4,
        out_specs=(vm, vm),
        scratch_shapes=[
            pltpu.VMEM((16, 16, 1024), F32),
            pltpu.VMEM((8, 8, 1024), F32),
            pltpu.VMEM((8, 8, 1024), F32),
            pltpu.VMEM((4, 16, 1024), F32),
            pltpu.VMEM((4, 16, 1024), F32),
            pltpu.VMEM((8, 8, 8, 128), F32),
            pltpu.VMEM((8, 8, 128), F32),
            pltpu.VMEM((16, 8, 128), F32),
            dma((8,)), dma((8,)), dma((16,)), dma((16,)),
        ]
        + [dma((4,))] * 8,
        compiler_params=pltpu.CompilerParams(
            collective_id=0, has_side_effects=True, vmem_limit_bytes=40 * 2**20
        ),
    )(y, up, down, r)


def shards(atom_cell, atom_frac, atom_weight, block_count, miller_h, miller_k, miller_l):
    y, up, down, r = local(
        atom_cell[:, 0], atom_frac[:, 0], atom_weight[0], block_count[0], miller_h, miller_k, miller_l
    )
    return exchange(y, up, down, r)


def solution(mesh):
    in_specs = (
        P(None, "gx", "gy", None, None),
        P(None, "gx", "gy", None, None),
        P("gx", "gy", None, None),
        P("gx", "gy", None),
        P(),
        P(),
        P(),
    )
    out_specs = (P("gx", "gy", None), P(("gx", "gy"), None))
    return jax.shard_map(shards, mesh=mesh, in_specs=in_specs, out_specs=out_specs, check_vma=False)
```

```python
import math

import jax
import jax.numpy as jnp
from jax import lax
from jax.experimental import pallas as pl
from jax.experimental.pallas import tpu as pltpu
from jax.sharding import PartitionSpec as P

SIGMA2 = 0.9 * 0.9
INV = 1.0 / SIGMA2
NORMAL = 1.0 / (0.9 * math.sqrt(2.0 * math.pi))
F32 = jnp.float32
BF16 = jnp.bfloat16
NT = (((1,), (1,)), ((), ()))
NN = (((1,), (0,)), ((), ()))
MESH = pl.DeviceIdType.MESH
TILE = 256


def iota(shape, dim):
    return lax.broadcasted_iota(jnp.int32, shape, dim)


def slot(row):
    return row - 4 if row >= 4 else row + 12


def slot_x(row):
    return row - 4 if row >= 4 else (row + 11 if row else 15)


def dense_taps(cell, frac, scale, out, tile, place, exact=False):
    u = cell.astype(F32) + (frac - 4.0)
    up = jnp.exp(u * INV)
    down = jnp.exp(u * (-INV))
    mid = jnp.exp(u * u * (-0.5 * INV)) * scale
    r = place(8)
    out[tile, 8 * r : 8 * r + 8, :] = mid
    below = [cell <= j for j in range(7)]
    p, q = mid, mid
    for k in range(1, 8):
        step = math.exp(-(2 * k - 1) * 0.5 * INV)
        p = p * (up * step) if exact else p * up
        q = q * (down * step) if exact else q * down
        r = place(8 + k)
        out[tile, 8 * r : 8 * r + 8, :] = jnp.where(below[k - 1], 0.0, p)
        r = place(8 - k)
        out[tile, 8 * r : 8 * r + 8, :] = jnp.where(below[7 - k], q, 0.0)


def crossed(x, y, tile, b):
    yy = y[tile, pl.ds(b, 16, stride=8), :].astype(BF16)
    parts = []
    for a in range(15):
        x8 = x[tile, pl.ds(a * 8 + b, 8, stride=0), :]
        parts.append(jnp.concatenate([x8, x8], 0).astype(BF16) * yy)
    return jnp.concatenate(parts + [jnp.zeros((16, 128), BF16)], 0)


def sincos(q, extent):
    eighth = extent // 8
    s = q + eighth
    quad = (s >> (extent.bit_length() - 3)) & 3
    r = ((s & (2 * eighth - 1)) - eighth).astype(F32) * (2.0 * math.pi / extent)
    r2 = r * r
    sin = r * (1.0 + r2 * (-1 / 6 + r2 * (1 / 120 + r2 * (-1 / 5040 + r2 * (1 / 362880)))))
    cos = 1.0 + r2 * (-0.5 + r2 * (1 / 24 + r2 * (-1 / 720 + r2 * (1 / 40320 + r2 * (-1 / 3628800)))))
    odd = (quad & 1) == 1
    c = jnp.where(odd, sin, cos)
    s = jnp.where(odd, cos, sin)
    c = jnp.where((quad == 1) | (quad == 2), -c, c)
    s = jnp.where(quad >= 2, -s, s)
    return c, s


def split(v):
    hi = v.astype(BF16)
    return hi, (v - hi.astype(F32)).astype(BF16)


def mm(a, b, dims=NN):
    return lax.dot_general(a, b, dims, preferred_element_type=F32)


def fused_kernel(
    cnt, cell, frac, w, mh, mk, ml,
    dens, inten,
    packed, fx, fy, fz, ws, xa, ya, za, xb, yb, zb, inner, edge, tab_hi, tab_lo, zsum, tt, d_hi, d_lo,
    amps, q, up_buf, down_buf, up_got, down_got, right_got, left_got, got1, part, got2,
    s1, g1, s2, g2, up_s, up_g, down_s, down_g, right_s, right_g, left_s, left_g,
):
    nx, ny = lax.axis_size("gx"), lax.axis_size("gy")
    me_x, me_y = lax.axis_index("gx"), lax.axis_index("gy")
    remote = nx > 1
    if remote:
        barrier = pltpu.get_barrier_semaphore()

        def greet_y(d, _):
            pl.semaphore_signal(barrier, inc=1, device_id=(me_x, (me_y + d) % ny), device_id_type=MESH)
            return 0

        def greet_x(d, _):
            pl.semaphore_signal(barrier, inc=1, device_id=((me_x + d) % nx, me_y), device_id_type=MESH)
            return 0

        lax.fori_loop(1, ny, greet_y, 0)
        lax.fori_loop(1, nx, greet_x, 0)

    def first(d, v):
        to = (me_y + d) % ny
        two = pl.ds(2 * v, 2)
        return pltpu.make_async_remote_copy(
            amps.at[to, two], got1.at[d, two], s1.at[v, d], g1.at[v, d], device_id=(me_x, to), device_id_type=MESH
        )

    def second(d):
        to = (me_x + d) % nx
        return pltpu.make_async_remote_copy(
            part.at[to // 2], got2.at[d], s2.at[d], g2.at[d], device_id=(to, me_y), device_id_type=MESH
        )

    def piece(src, dst, ss, gs, t, to):
        z = pl.ds(pl.multiple_of(t * TILE, TILE), TILE)
        return pltpu.make_async_remote_copy(
            src.at[:, :, z], dst.at[:, :, z], ss.at[t], gs.at[t], device_id=to, device_id_type=MESH
        )

    def ups(t):
        return piece(up_buf, up_got, up_s, up_g, t, (me_x, (me_y + 1) % ny))

    def downs(t):
        return piece(down_buf, down_got, down_s, down_g, t, (me_x, (me_y + ny - 1) % ny))

    def rights(t):
        return piece(q.at[pl.ds(8, 4)], right_got, right_s, right_g, t, ((me_x + 1) % nx, me_y))

    def lefts(t):
        return piece(q.at[pl.ds(12, 3)], left_got, left_s, left_g, t, ((me_x + nx - 1) % nx, me_y))

    def pieces(fn, out):
        for t in range(9):
            if t < 8:
                v = fn(t // 4, 128 * (t % 4), 128)
            else:
                v = jnp.concatenate([fn(0, 512, 64), fn(1, 512, 64)], 0)
            out[t] = v.T

    pieces(lambda c, s, n: cell[0, c, s : s + n] + cell[1, c, s : s + n] * 8 + cell[2, c, s : s + n] * 64, packed)
    for d, o in ((0, fx), (1, fy), (2, fz)):
        pieces(lambda c, s, n: frac[d, c, s : s + n], o)

    def weigh(c, s, n):
        taken = iota((n, 128), 0) + s < cnt[c : c + 1, :]
        return jnp.where(taken, w[c, s : s + n] * NORMAL, 0.0)

    pieces(weigh, ws)
    for o in (ya, za, yb, zb):
        for t in range(9):
            o[t, 96:104, :] = jnp.zeros((8, 128), F32)

    row8 = iota((8, 128), 0)
    lcol = jnp.concatenate([ml[v // 2] + (row8 + 8 * (v % 2) - 8) for v in range(16)], 0)
    c0, s0 = sincos((lcol * iota((128, 128), 1)) & 1023, 1024)
    cw, sw = sincos((lcol * 128) & 1023, 1024)
    for t in range(8):
        for half, v in ((0, c0), (1, -s0)):
            hi, lo = split(v)
            tab_hi[128 * half : 128 * half + 128, 128 * t : 128 * t + 128] = hi
            tab_lo[128 * half : 128 * half + 128, 128 * t : 128 * t + 128] = lo
        c0, s0 = c0 * cw - s0 * sw, s0 * cw + c0 * sw
    zsum[...] = jnp.zeros_like(zsum)

    def dense(g, t, taps):
        gs = pl.ds(pl.multiple_of(g * 8, 8), 8)
        p = packed[t, gs, :]
        dense_taps(p & 7, fx[t, gs, :], 1.0, taps[0], t, slot_x)
        dense_taps((p >> 3) & 7, fy[t, gs, :], 1.0, taps[1], t, slot)
        dense_taps(p >> 6, fz[t, gs, :], ws[t, gs, :], taps[2], t, slot, exact=True)

    lane16 = iota((16, 128), 1)

    def group(g, taps):
        xs, ys, zs = taps
        for t in (8, 0, 2, 4, 6):
            dense(g, t, taps)
            if t < 8:
                dense(g, t + 1, taps)
            for b in range(8):
                base = pl.multiple_of(g * 64 + b * 8, 8)
                here, there = pl.ds(base, 8), pl.ds(base + 8, 8)
                if t == 8:
                    zt = zs[8, pl.ds(b, 16, stride=8), :]
                    zm = jnp.concatenate([jnp.where(lane16 < 64, zt, 0.0), jnp.where(lane16 < 64, 0.0, zt)], 0)
                    f = mm(zm.astype(BF16), crossed(xs, ys, 8, b), NT)
                    for c in range(2):
                        inner[c, here, :] = f[16 * c : 16 * c + 8]
                        edge[c, there, :] = f[16 * c + 8 : 16 * c + 16]
                else:
                    zz = jnp.concatenate([zs[t + e, pl.ds(b, 16, stride=8), :] for e in (0, 1)], 1).astype(BF16)
                    cc = jnp.concatenate([crossed(xs, ys, t + e, b) for e in (0, 1)], 1)
                    f = mm(zz, cc, NT)
                    inner[t // 4, here, :] += f[0:8]
                    edge[t // 4, there, :] += f[8:16]

    taps_a, taps_b = (xa, ya, za), (xb, yb, zb)

    def groups(i, _):
        group((2 * i + 15) & 15, taps_a)
        group((2 * i) & 15, taps_b)
        return 0

    low256 = (iota((TILE, 256), 0) & 7) < 4
    lane = iota((8, 256), 1)
    k2 = jnp.zeros((8, 256), F32)
    for row in range(1, 16):
        square = float((row - 8) ** 2)
        k2 = k2 + jnp.where((lane >> 4) == slot_x(row), square, 0.0) + jnp.where((lane & 15) == slot(row), square, 0.0)
    gain = jnp.exp(k2 * (-0.5 * INV)) * (NORMAL * NORMAL)
    low = iota((8, TILE), 0) < 4

    def density_tile(t):
        z0 = pl.multiple_of(t * TILE, TILE)
        z = pl.ds(z0, TILE)
        spread = lambda v: jnp.concatenate([v] * (TILE // 8), 0)
        for c in range(2):
            beyond = jnp.where(low256, edge[c, z, :], edge[c, pl.ds(z0 + 16, TILE), :])
            d = (inner[c, z, :] + beyond) * spread(gain)
            tt[c] = d.T
            hi, lo = split(d)
            d_hi[...] = hi
            d_lo[...] = lo
            th = tab_hi[:, z]
            tl = tab_lo[:, z]
            zsum[c] += mm(th, d_hi[...]) + mm(th, d_lo[...]) + mm(tl, d_hi[...])
        for k in range(8):
            tops, bottoms = [], []
            for a in (2 * k, 2 * k + 1):
                in0, out0 = tt[0, 16 * a : 16 * a + 8, :], tt[0, 16 * a + 8 : 16 * a + 16, :]
                in1, out1 = tt[1, 16 * a : 16 * a + 8, :], tt[1, 16 * a + 8 : 16 * a + 16, :]
                q[a, 0:8, z] = in0 + jnp.where(low, 0.0, out1)
                q[a, 8:16, z] = in1 + jnp.where(low, out0, 0.0)
                tops.append(out1)
                bottoms.append(out0)
            up_buf[k, :, z] = jnp.where(low, tops[0], pltpu.roll(tops[1], 4, 0))
            down_buf[k, :, z] = jnp.where(low, pltpu.roll(bottoms[0], 4, 0), bottoms[1])

    def fold_y(t):
        z = pl.ds(pl.multiple_of(t * TILE, TILE), TILE)
        for k in (4, 5, 6, 7, 0, 1, 2, 3):
            a = 2 * k
            u, d = up_got[k, :, z], down_got[k, :, z]
            q[a, 0:8, z] += jnp.where(low, u, 0.0)
            q[a + 1, 0:8, z] += jnp.where(low, pltpu.roll(u, 4, 0), 0.0)
            q[a, 8:16, z] += jnp.where(low, 0.0, pltpu.roll(d, 4, 0))
            q[a + 1, 8:16, z] += jnp.where(low, 0.0, d)

    def pass_on(t):
        if remote:
            ups(t).wait()
            downs(t).wait()
        fold_y(t)
        if remote:
            rights(t).start()
            lefts(t).start()

    def tiles(t, _):
        lax.fori_loop(jnp.where(t == 0, 0, 2 * t + 1), jnp.where(t == 3, 8, 2 * t + 3), groups, 0)

        @pl.when(t == 0)
        def _():
            for c in range(2):
                edge[c, 0:8, :] = edge[c, 1024:1032, :]

        @pl.when(t == 3)
        def _():
            for c in range(2):
                edge[c, 1032:1040, :] = edge[c, 8:16, :]

        density_tile(t)
        if remote:

            @pl.when(t == 0)
            def _():
                pl.semaphore_wait(barrier, nx + ny - 2)

            ups(t).start()
            downs(t).start()

        @pl.when(t > 0)
        def _():
            pass_on(t - 1)

        return 0

    lax.fori_loop(0, 4, tiles, 0)

    x0 = me_x * 8
    y0 = me_y * 16
    n = iota((16, 256), 1)
    ip = (n & 63) >> 2
    ni = (ip & 1) * 8 + (ip >> 1) - 8
    nj = (n >> 6) * 4 + (n & 3) - 8
    off = iota((16, 256), 0)
    off_x = jnp.where(off < 12, off, off - 15)
    off_y = jnp.where(off < 12, off, off - 16)
    lane_low = iota((16, 128), 1) < 64

    def pair(v, _):
        us = []
        for e in range(2):
            win = 2 * v + e
            hx = mh[win] + ni
            ky = mk[win] + nj
            xr, xi = sincos((hx * (x0 + off_x)) & 127, 128)
            yr, yi = sincos((ky * (y0 + off_y)) & 127, 128)
            pr, pi = sincos((ky[0:1] * 8) & 127, 128)
            mr, mi = [], []
            for a in range(16):
                mr.append(xr[a : a + 1] * yr - xi[a : a + 1] * yi)
                mi.append(-(xr[a : a + 1] * yi + xi[a : a + 1] * yr))
            mrh, mrl = split(jnp.concatenate(mr, 0))
            mih, mil = split(jnp.concatenate(mi, 0))
            rows = [
                zsum[c, pl.ds(pl.multiple_of(128 * half + win * 16, 16), 16), :] for c in (0, 1) for half in (0, 1)
            ]
            zh, zl = split(jnp.concatenate(rows, 0))
            A = mm(zh, mrh) + mm(zl, mrh) + mm(zh, mrl)
            B = mm(zh, mih) + mm(zl, mih) + mm(zh, mil)
            re0, im0 = A[0:16] - B[16:32], A[16:32] + B[0:16]
            re1, im1 = A[32:48] - B[48:64], A[48:64] + B[32:48]
            us.append((re0 + re1 * pr + im1 * pi, im0 + im1 * pr - re1 * pi))
        rows = []
        for jh in range(4):
            for half in range(2):
                a0 = us[0][half][:, 128 * (jh // 2) : 128 * (jh // 2) + 128]
                a1 = us[1][half][:, 128 * (jh // 2) : 128 * (jh // 2) + 128]
                if jh % 2 == 0:
                    rows.append(jnp.where(lane_low, a0, pltpu.roll(a1, 64, 1)))
                else:
                    rows.append(jnp.where(lane_low, pltpu.roll(a0, 64, 1), a1))
        tr = jnp.concatenate(rows, 0).T
        for e in range(2):
            for il in range(8):
                amps[il, 2 * v + e] = tr[64 * e + 8 * il : 64 * e + 8 * il + 8]
        if remote:

            def send(d, _):
                first(d, v).start()
                return 0

            lax.fori_loop(1, ny, send, 0)
        return 0

    lax.fori_loop(0, 4, pair, 0)
    pass_on(3)

    if not remote:
        dens[...] = q[0:8]
        inten[...] = amps[0, 0, 0:1, :]
        return

    def finish_first(i, _):
        first(1 + i // 4, i % 4).wait()
        return 0

    lax.fori_loop(0, 4 * (ny - 1), finish_first, 0)
    part[...] = amps[me_y] + lax.fori_loop(2, ny, lambda d, s: s + got1[d], got1[1])

    def send_second(d, _):
        second(d).start()
        return 0

    def finish_second(d, _):
        second(d).wait()
        return 0

    lax.fori_loop(1, nx, send_second, 0)
    lax.fori_loop(1, nx, finish_second, 0)
    total = part[me_x // 2] + lax.fori_loop(2, nx, lambda d, s: s + got2[d], got2[1])
    odd = (iota((8, 128), 0) * 0 + me_x % 2) == 1
    mine = jnp.where(odd, pltpu.roll(total, 4, 0), total)
    power = mine * mine
    power = power + pltpu.roll(power, 112, 1)
    n = iota((128, 256), 1)
    pick = (iota((128, 256), 0) == (n >> 6) * 32 + (n & 15)).astype(F32)
    wide = lax.dot_general(power, pick, NN, precision=lax.Precision.HIGHEST, preferred_element_type=F32)
    keep = iota((8, 256), 0) == ((iota((8, 256), 1) >> 4) & 3)
    inten[...] = jnp.sum(jnp.where(keep, wide, 0.0), axis=0, keepdims=True) * (1.0 / 16777216.0)

    for t in range(4):
        z = slice(t * TILE, t * TILE + TILE)
        rights(t).wait()
        lefts(t).wait()
        dens[0:4, :, z] = q[0:4, :, z] + right_got[:, :, z]
        dens[4:5, :, z] = q[4:5, :, z]
        dens[5:8, :, z] = q[5:8, :, z] + left_got[:, :, z]


def local(cell, frac, w, cnt, mh, mk, ml):
    cell = jnp.swapaxes(cell, 2, 3)
    frac = jnp.swapaxes(frac, 2, 3)
    w = jnp.swapaxes(w, 1, 2)
    vm = pl.BlockSpec(memory_space=pltpu.VMEM)
    sm = pl.BlockSpec(memory_space=pltpu.SMEM)
    sd = jax.ShapeDtypeStruct
    vmem = pltpu.VMEM
    dma = pltpu.SemaphoreType.DMA
    multi = lax.axis_size("gx") > 1
    return pl.pallas_call(
        fused_kernel,
        out_shape=(sd((8, 16, 1024), F32), sd((1, 256 if multi else 128), F32)),
        in_specs=[vm] * 4 + [sm] * 3,
        out_specs=(vm, vm),
        scratch_shapes=[vmem((9, 128, 128), jnp.int32)]
        + [vmem((9, 128, 128), F32)] * 10
        + [
            vmem((2, 1024, 256), F32),
            vmem((2, 1040, 256), F32),
            vmem((256, 1024), BF16),
            vmem((256, 1024), BF16),
            vmem((2, 256, 256), F32),
            vmem((2, 256, TILE), F32),
            vmem((TILE, 256), BF16),
            vmem((TILE, 256), BF16),
            vmem((8, 8, 8, 128), F32),
            vmem((16, 16, 1024), F32),
            vmem((8, 8, 1024), F32),
            vmem((8, 8, 1024), F32),
            vmem((8, 8, 1024), F32),
            vmem((8, 8, 1024), F32),
            vmem((4, 16, 1024), F32),
            vmem((3, 16, 1024), F32),
            vmem((8, 8, 8, 128), F32),
            vmem((8, 8, 128), F32),
            vmem((16, 8, 128), F32),
            dma((4, 8)), dma((4, 8)), dma((16,)), dma((16,)),
        ]
        + [dma((4,))] * 8,
        compiler_params=pltpu.CompilerParams(
            collective_id=0 if multi else None, has_side_effects=True, vmem_limit_bytes=60 * 2**20
        ),
    )(cnt, cell, frac, w, mh, mk, ml)


def shards(atom_cell, atom_frac, atom_weight, block_count, miller_h, miller_k, miller_l):
    return local(atom_cell[:, 0], atom_frac[:, 0], atom_weight[0], block_count[0], miller_h, miller_k, miller_l)


def solution(mesh):
    in_specs = (
        P(None, "gx", "gy", None, None),
        P(None, "gx", "gy", None, None),
        P("gx", "gy", None, None),
        P("gx", "gy", None),
        P(),
        P(),
        P(),
    )
    out_specs = (P("gx", "gy", None), P(("gx", "gy"), None))
    return jax.shard_map(shards, mesh=mesh, in_specs=in_specs, out_specs=out_specs, check_vma=False)
```

```python
import math

import jax
import jax.numpy as jnp
from jax import lax
from jax.experimental import pallas as pl
from jax.experimental.pallas import tpu as pltpu
from jax.sharding import PartitionSpec as P

SIGMA2 = 0.9 * 0.9
INV = 1.0 / SIGMA2
NORMAL = 1.0 / (0.9 * math.sqrt(2.0 * math.pi))
F32 = jnp.float32
BF16 = jnp.bfloat16
NT = (((1,), (1,)), ((), ()))
NN = (((1,), (0,)), ((), ()))
MESH = pl.DeviceIdType.MESH
TILE = 256


def iota(shape, dim):
    return lax.broadcasted_iota(jnp.int32, shape, dim)


def slot(row):
    return row - 4 if row >= 4 else row + 12


def slot_x(row):
    return row - 4 if row >= 4 else (row + 11 if row else 15)


def dense_taps(cell, frac, scale, out, tile, place, exact=False):
    u = cell.astype(F32) + (frac - 4.0)
    up = jnp.exp(u * INV)
    down = jnp.exp(u * (-INV))
    mid = jnp.exp(u * u * (-0.5 * INV)) * scale
    r = place(8)
    out[tile, 8 * r : 8 * r + 8, :] = mid
    below = [cell <= j for j in range(7)]
    p, q = mid, mid
    for k in range(1, 8):
        step = math.exp(-(2 * k - 1) * 0.5 * INV)
        p = p * (up * step) if exact else p * up
        q = q * (down * step) if exact else q * down
        r = place(8 + k)
        out[tile, 8 * r : 8 * r + 8, :] = jnp.where(below[k - 1], 0.0, p)
        r = place(8 - k)
        out[tile, 8 * r : 8 * r + 8, :] = jnp.where(below[7 - k], q, 0.0)


def crossed(x, y, tile, b):
    yy = y[tile, pl.ds(b, 16, stride=8), :].astype(BF16)
    parts = []
    for a in range(15):
        x8 = x[tile, pl.ds(a * 8 + b, 8, stride=0), :]
        parts.append(jnp.concatenate([x8, x8], 0).astype(BF16) * yy)
    return jnp.concatenate(parts + [jnp.zeros((16, 128), BF16)], 0)


def sincos(q, extent):
    eighth = extent // 8
    s = q + eighth
    quad = (s >> (extent.bit_length() - 3)) & 3
    r = ((s & (2 * eighth - 1)) - eighth).astype(F32) * (2.0 * math.pi / extent)
    r2 = r * r
    sin = r * (1.0 + r2 * (-1 / 6 + r2 * (1 / 120 + r2 * (-1 / 5040 + r2 * (1 / 362880)))))
    cos = 1.0 + r2 * (-0.5 + r2 * (1 / 24 + r2 * (-1 / 720 + r2 * (1 / 40320 + r2 * (-1 / 3628800)))))
    odd = (quad & 1) == 1
    c = jnp.where(odd, sin, cos)
    s = jnp.where(odd, cos, sin)
    c = jnp.where((quad == 1) | (quad == 2), -c, c)
    s = jnp.where(quad >= 2, -s, s)
    return c, s


def split(v):
    hi = v.astype(BF16)
    return hi, (v - hi.astype(F32)).astype(BF16)


def mm(a, b, dims=NN):
    return lax.dot_general(a, b, dims, preferred_element_type=F32)


def fused_kernel(
    cnt, cell_in, frac_in, w_in, mh, mk, ml,
    dens, inten,
    cell, frac, w, in_sem,
    packed, fx, fy, fz, ws, xa, ya, za, xb, yb, zb, side_a, side_b, inner, edge, tab_hi, tab_lo, zsum, tt, d_hi, d_lo,
    amps, q, up_buf, down_buf, up_got, down_got, right_got, left_got, got1, part, got2,
    s1, g1, s2, g2, up_s, up_g, down_s, down_g, right_s, right_g, left_s, left_g,
):
    nx, ny = lax.axis_size("gx"), lax.axis_size("gy")
    me_x, me_y = lax.axis_index("gx"), lax.axis_index("gy")
    remote = nx > 1
    loads = [pltpu.make_async_copy(cell_in, cell, in_sem.at[0])]
    loads += [pltpu.make_async_copy(frac_in.at[d], frac.at[d], in_sem.at[1 + d]) for d in range(3)]
    loads += [pltpu.make_async_copy(w_in, w, in_sem.at[4])]
    for load in loads:
        load.start()
    if remote:
        barrier = pltpu.get_barrier_semaphore()

        def greet_y(d, _):
            pl.semaphore_signal(barrier, inc=1, device_id=(me_x, (me_y + d) % ny), device_id_type=MESH)
            return 0

        def greet_x(d, _):
            pl.semaphore_signal(barrier, inc=1, device_id=((me_x + d) % nx, me_y), device_id_type=MESH)
            return 0

        lax.fori_loop(1, ny, greet_y, 0)
        lax.fori_loop(1, nx, greet_x, 0)

    def first(d, v):
        to = (me_y + d) % ny
        two = pl.ds(2 * v, 2)
        return pltpu.make_async_remote_copy(
            amps.at[to, two], got1.at[d, two], s1.at[v, d], g1.at[v, d], device_id=(me_x, to), device_id_type=MESH
        )

    def second(d):
        to = (me_x + d) % nx
        return pltpu.make_async_remote_copy(
            part.at[to // 2], got2.at[d], s2.at[d], g2.at[d], device_id=(to, me_y), device_id_type=MESH
        )

    def piece(src, dst, ss, gs, t, to):
        z = pl.ds(pl.multiple_of(t * TILE, TILE), TILE)
        return pltpu.make_async_remote_copy(
            src.at[:, :, z], dst.at[:, :, z], ss.at[t], gs.at[t], device_id=to, device_id_type=MESH
        )

    def ups(t):
        return piece(up_buf, up_got, up_s, up_g, t, (me_x, (me_y + 1) % ny))

    def downs(t):
        return piece(down_buf, down_got, down_s, down_g, t, (me_x, (me_y + ny - 1) % ny))

    def rights(t):
        return piece(q.at[pl.ds(8, 4)], right_got, right_s, right_g, t, ((me_x + 1) % nx, me_y))

    def lefts(t):
        return piece(q.at[pl.ds(12, 3)], left_got, left_s, left_g, t, ((me_x + nx - 1) % nx, me_y))

    row8 = iota((8, 128), 0)
    lcol = jnp.concatenate([ml[v // 2] + (row8 + 8 * (v % 2) - 8) for v in range(16)], 0)
    c0, s0 = sincos((lcol * iota((128, 128), 1)) & 1023, 1024)
    cw, sw = sincos((lcol * 128) & 1023, 1024)
    for t in range(8):
        for half, v in ((0, c0), (1, -s0)):
            hi, lo = split(v)
            tab_hi[128 * half : 128 * half + 128, 128 * t : 128 * t + 128] = hi
            tab_lo[128 * half : 128 * half + 128, 128 * t : 128 * t + 128] = lo
        c0, s0 = c0 * cw - s0 * sw, s0 * cw + c0 * sw
    zsum[...] = jnp.zeros_like(zsum)

    for o in (ya, za, yb, zb):
        for t in range(9):
            o[t, 96:104, :] = jnp.zeros((8, 128), F32)

    def pieces(fn, out):
        for t in range(9):
            if t < 8:
                v = fn(t // 4, 128 * (t % 4), 128)
            else:
                v = jnp.concatenate([fn(0, 512, 64), fn(1, 512, 64)], 0)
            out[t] = v.T

    loads[0].wait()
    pieces(lambda c, s, n: cell[0, c, s : s + n] + cell[1, c, s : s + n] * 8 + cell[2, c, s : s + n] * 64, packed)
    for d, o in ((0, fx), (1, fy), (2, fz)):
        loads[1 + d].wait()
        pieces(lambda c, s, n: frac[d, c, s : s + n], o)

    def weigh(c, s, n):
        taken = iota((n, 128), 0) + s < cnt[c : c + 1, :]
        return jnp.where(taken, w[c, s : s + n] * NORMAL, 0.0)

    loads[4].wait()
    pieces(weigh, ws)
    x0 = me_x * 8
    y0 = me_y * 16
    n = iota((16, 256), 1)
    ip = (n & 63) >> 2
    ni = (ip & 1) * 8 + (ip >> 1) - 8
    nj = (n >> 6) * 4 + (n & 3) - 8
    off = iota((16, 256), 0)
    off_x = jnp.where(off < 12, off, off - 15)
    off_y = jnp.where(off < 12, off, off - 16)

    def dense(g, t, taps):
        gs = pl.ds(pl.multiple_of(g * 8, 8), 8)
        p = packed[t, gs, :]
        dense_taps(p & 7, fx[t, gs, :], 1.0, taps[0], t, slot_x)
        dense_taps((p >> 3) & 7, fy[t, gs, :], 1.0, taps[1], t, slot)
        dense_taps(p >> 6, fz[t, gs, :], ws[t, gs, :], taps[2], t, slot, exact=True)

    lane16 = iota((16, 128), 1)

    def group(g, taps, side):
        xs, ys, zs = taps
        for t in range(9):
            dense(g, t, taps)

        def wide(ts, b):
            zz = jnp.concatenate([zs[t, pl.ds(b, 16, stride=8), :] for t in ts], 1).astype(BF16)
            return zz, jnp.concatenate([crossed(xs, ys, t, b) for t in ts], 1)

        for b in range(8):
            base = pl.multiple_of(g * 64 + b * 8, 8)
            here, there = pl.ds(base, 8), pl.ds(base + 8, 8)
            zt = zs[8, pl.ds(b, 16, stride=8), :]
            zm = jnp.concatenate([jnp.where(lane16 < 64, zt, 0.0), jnp.where(lane16 < 64, 0.0, zt)], 0)
            zz, cc = wide((4, 5), b)
            st = mm(cc, zz, NT)
            fm = mm(zm.astype(BF16), crossed(xs, ys, 8, b), NT)
            zz, cc = wide((0, 1), b)
            f = fm[0:16] + mm(zz, cc, NT)
            zz, cc = wide((6, 7), b)
            st = st + mm(cc, zz, NT)
            zz, cc = wide((2, 3), b)
            f = f + mm(zz, cc, NT)
            side[:, 16 * b : 16 * b + 16] = st
            inner[0, here, :] = f[0:8]
            edge[0, there, :] = f[8:16]
            inner[1, here, :] = fm[16:24]
            edge[1, there, :] = fm[24:32]

        tr = side[...].T
        for b in range(8):
            base = pl.multiple_of(g * 64 + b * 8, 8)
            inner[1, pl.ds(base, 8), :] += tr[16 * b : 16 * b + 8]
            edge[1, pl.ds(base + 8, 8), :] += tr[16 * b + 8 : 16 * b + 16]

    taps_a, taps_b = (xa, ya, za), (xb, yb, zb)

    def groups(i, _):
        group((2 * i + 15) & 15, taps_a, side_a)
        group((2 * i) & 15, taps_b, side_b)
        return 0

    low256 = (iota((TILE, 256), 0) & 7) < 4
    lane = iota((8, 256), 1)
    k2 = jnp.zeros((8, 256), F32)
    for row in range(1, 16):
        square = float((row - 8) ** 2)
        k2 = k2 + jnp.where((lane >> 4) == slot_x(row), square, 0.0) + jnp.where((lane & 15) == slot(row), square, 0.0)
    gain = jnp.exp(k2 * (-0.5 * INV)) * (NORMAL * NORMAL)
    low = iota((8, TILE), 0) < 4

    def density_tile(t):
        z0 = pl.multiple_of(t * TILE, TILE)
        z = pl.ds(z0, TILE)
        spread = lambda v: jnp.concatenate([v] * (TILE // 8), 0)
        for c in range(2):
            beyond = jnp.where(low256, edge[c, z, :], edge[c, pl.ds(z0 + 16, TILE), :])
            d = (inner[c, z, :] + beyond) * spread(gain)
            tt[c] = d.T
            hi, lo = split(d)
            d_hi[...] = hi
            d_lo[...] = lo
            th = tab_hi[:, z]
            tl = tab_lo[:, z]
            zsum[c] += mm(th, d_hi[...]) + mm(th, d_lo[...]) + mm(tl, d_hi[...])

    def assemble(t):
        z = pl.ds(pl.multiple_of(t * TILE, TILE), TILE)
        for k in range(8):
            tops, bottoms = [], []
            for a in (2 * k, 2 * k + 1):
                in0, out0 = tt[0, 16 * a : 16 * a + 8, :], tt[0, 16 * a + 8 : 16 * a + 16, :]
                in1, out1 = tt[1, 16 * a : 16 * a + 8, :], tt[1, 16 * a + 8 : 16 * a + 16, :]
                q[a, 0:8, z] = in0 + jnp.where(low, 0.0, out1)
                q[a, 8:16, z] = in1 + jnp.where(low, out0, 0.0)
                tops.append(out1)
                bottoms.append(out0)
            up_buf[k, :, z] = jnp.where(low, tops[0], pltpu.roll(tops[1], 4, 0))
            down_buf[k, :, z] = jnp.where(low, pltpu.roll(bottoms[0], 4, 0), bottoms[1])

    def fold_y(t):
        z = pl.ds(pl.multiple_of(t * TILE, TILE), TILE)
        for k in (4, 5, 6, 7, 0, 1, 2, 3):
            a = 2 * k
            u, d = up_got[k, :, z], down_got[k, :, z]
            q[a, 0:8, z] += jnp.where(low, u, 0.0)
            q[a + 1, 0:8, z] += jnp.where(low, pltpu.roll(u, 4, 0), 0.0)
            q[a, 8:16, z] += jnp.where(low, 0.0, pltpu.roll(d, 4, 0))
            q[a + 1, 8:16, z] += jnp.where(low, 0.0, d)

    def pass_on(t):
        if remote:
            ups(t).wait()
            downs(t).wait()
        fold_y(t)
        if remote:
            rights(t).start()
            lefts(t).start()

    def tiles(t, _):
        lax.fori_loop(jnp.where(t == 0, 0, 2 * t + 1), jnp.where(t == 3, 8, 2 * t + 3), groups, 0)

        @pl.when(t == 0)
        def _():
            for c in range(2):
                edge[c, 0:8, :] = edge[c, 1024:1032, :]

        @pl.when(t == 3)
        def _():
            for c in range(2):
                edge[c, 1032:1040, :] = edge[c, 8:16, :]

        density_tile(t)

        @pl.when(t < 3)
        def _():
            assemble(t)
            if remote:

                @pl.when(t == 0)
                def _():
                    pl.semaphore_wait(barrier, nx + ny - 2)

                ups(t).start()
                downs(t).start()

            @pl.when(t > 0)
            def _():
                pass_on(t - 1)

        return 0

    lax.fori_loop(0, 4, tiles, 0)

    lane_low = iota((16, 128), 1) < 64

    def pair(v, _):
        us = []
        for e in range(2):
            win = 2 * v + e
            pr, pi = sincos(((mk[win] + nj[0:1]) * 8) & 127, 128)
            xr, xi = sincos(((mh[win] + ni) * (x0 + off_x)) & 127, 128)
            yr, yi = sincos(((mk[win] + nj) * (y0 + off_y)) & 127, 128)
            mr, mi = [], []
            for a in range(16):
                mr.append(xr[a : a + 1] * yr - xi[a : a + 1] * yi)
                mi.append(-(xr[a : a + 1] * yi + xi[a : a + 1] * yr))
            mrh, mrl = split(jnp.concatenate(mr, 0))
            mih, mil = split(jnp.concatenate(mi, 0))
            rows = [
                zsum[c, pl.ds(pl.multiple_of(128 * half + win * 16, 16), 16), :] for c in (0, 1) for half in (0, 1)
            ]
            zh, zl = split(jnp.concatenate(rows, 0))
            A = mm(zh, mrh) + mm(zl, mrh) + mm(zh, mrl)
            B = mm(zh, mih) + mm(zl, mih) + mm(zh, mil)
            re0, im0 = A[0:16] - B[16:32], A[16:32] + B[0:16]
            re1, im1 = A[32:48] - B[48:64], A[48:64] + B[32:48]
            us.append((re0 + re1 * pr + im1 * pi, im0 + im1 * pr - re1 * pi))
        rows = []
        for jh in range(4):
            for half in range(2):
                a0 = us[0][half][:, 128 * (jh // 2) : 128 * (jh // 2) + 128]
                a1 = us[1][half][:, 128 * (jh // 2) : 128 * (jh // 2) + 128]
                if jh % 2 == 0:
                    rows.append(jnp.where(lane_low, a0, pltpu.roll(a1, 64, 1)))
                else:
                    rows.append(jnp.where(lane_low, pltpu.roll(a0, 64, 1), a1))
        tr = jnp.concatenate(rows, 0).T
        for e in range(2):
            for il in range(8):
                amps[il, 2 * v + e] = tr[64 * e + 8 * il : 64 * e + 8 * il + 8]
        if remote:

            def send(d, _):
                first(d, v).start()
                return 0

            lax.fori_loop(1, ny, send, 0)
        return 0

    lax.fori_loop(0, 4, pair, 0)
    assemble(3)
    if remote:
        ups(3).start()
        downs(3).start()
    pass_on(2)

    if not remote:
        pass_on(3)
        dens[...] = q[0:8]
        inten[...] = amps[0, 0, 0:1, :]
        return

    def finish_first(i, _):
        first(1 + i // 4, i % 4).wait()
        return 0

    lax.fori_loop(0, 4 * (ny - 1), finish_first, 0)
    own = amps[me_y]
    for d in range(1, 8):
        own = own + got1[d]
    part[...] = own

    def send_second(d, _):
        second(d).start()
        return 0

    def finish_second(d, _):
        second(d).wait()
        return 0

    lax.fori_loop(1, nx, send_second, 0)
    n = iota((128, 256), 1)
    pick = (iota((128, 256), 0) == (n >> 6) * 32 + (n & 15)).astype(F32)
    keep = iota((8, 256), 0) == ((iota((8, 256), 1) >> 4) & 3)
    odd = (iota((8, 128), 0) * 0 + me_x % 2) == 1
    pass_on(3)
    lax.fori_loop(1, nx, finish_second, 0)
    total = part[me_x // 2]
    for d in range(1, 16):
        total = total + got2[d]
    mine = jnp.where(odd, pltpu.roll(total, 4, 0), total)
    power = mine * mine
    power = power + pltpu.roll(power, 112, 1)
    wide = lax.dot_general(power, pick, NN, precision=lax.Precision.HIGHEST, preferred_element_type=F32)
    inten[...] = jnp.sum(jnp.where(keep, wide, 0.0), axis=0, keepdims=True) * (1.0 / 16777216.0)

    for t in range(4):
        z = slice(t * TILE, t * TILE + TILE)
        rights(t).wait()
        lefts(t).wait()
        dens[0:4, :, z] = q[0:4, :, z] + right_got[:, :, z]
        dens[4:5, :, z] = q[4:5, :, z]
        dens[5:8, :, z] = q[5:8, :, z] + left_got[:, :, z]


def local(cell, frac, w, cnt, mh, mk, ml):
    cell = jnp.swapaxes(cell, 2, 3)
    frac = jnp.swapaxes(frac, 2, 3)
    w = jnp.swapaxes(w, 1, 2)
    vm = pl.BlockSpec(memory_space=pltpu.VMEM)
    sm = pl.BlockSpec(memory_space=pltpu.SMEM)
    hbm = pl.BlockSpec(memory_space=pltpu.HBM)
    sd = jax.ShapeDtypeStruct
    vmem = pltpu.VMEM
    dma = pltpu.SemaphoreType.DMA
    multi = lax.axis_size("gx") > 1
    return pl.pallas_call(
        fused_kernel,
        out_shape=(sd((8, 16, 1024), F32), sd((1, 256 if multi else 128), F32)),
        in_specs=[vm] + [hbm] * 3 + [sm] * 3,
        out_specs=(vm, vm),
        scratch_shapes=[
            vmem((3, 2, 576, 128), jnp.int32),
            vmem((3, 2, 576, 128), F32),
            vmem((2, 576, 128), F32),
            dma((5,)),
            vmem((9, 128, 128), jnp.int32),
        ]
        + [vmem((9, 128, 128), F32)] * 10
        + [
            vmem((256, 128), F32),
            vmem((256, 128), F32),
            vmem((2, 1024, 256), F32),
            vmem((2, 1040, 256), F32),
            vmem((256, 1024), BF16),
            vmem((256, 1024), BF16),
            vmem((2, 256, 256), F32),
            vmem((2, 256, TILE), F32),
            vmem((TILE, 256), BF16),
            vmem((TILE, 256), BF16),
            vmem((8, 8, 8, 128), F32),
            vmem((16, 16, 1024), F32),
            vmem((8, 8, 1024), F32),
            vmem((8, 8, 1024), F32),
            vmem((8, 8, 1024), F32),
            vmem((8, 8, 1024), F32),
            vmem((4, 16, 1024), F32),
            vmem((3, 16, 1024), F32),
            vmem((8, 8, 8, 128), F32),
            vmem((8, 8, 128), F32),
            vmem((16, 8, 128), F32),
            dma((4, 8)), dma((4, 8)), dma((16,)), dma((16,)),
        ]
        + [dma((4,))] * 8,
        compiler_params=pltpu.CompilerParams(
            collective_id=0 if multi else None, has_side_effects=True, vmem_limit_bytes=58 * 2**20
        ),
    )(cnt, cell, frac, w, mh, mk, ml)


def shards(atom_cell, atom_frac, atom_weight, block_count, miller_h, miller_k, miller_l):
    return local(atom_cell[:, 0], atom_frac[:, 0], atom_weight[0], block_count[0], miller_h, miller_k, miller_l)


def solution(mesh):
    in_specs = (
        P(None, "gx", "gy", None, None),
        P(None, "gx", "gy", None, None),
        P("gx", "gy", None, None),
        P("gx", "gy", None),
        P(),
        P(),
        P(),
    )
    out_specs = (P("gx", "gy", None), P(("gx", "gy"), None))
    return jax.shard_map(shards, mesh=mesh, in_specs=in_specs, out_specs=out_specs, check_vma=False)
```

```python
import math

import jax
import jax.numpy as jnp
from jax import lax
from jax.experimental import pallas as pl
from jax.experimental.pallas import tpu as pltpu
from jax.sharding import PartitionSpec as P

SIGMA2 = 0.9 * 0.9
INV = 1.0 / SIGMA2
NORMAL = 1.0 / (0.9 * math.sqrt(2.0 * math.pi))
F32 = jnp.float32
BF16 = jnp.bfloat16
NT = (((1,), (1,)), ((), ()))
NN = (((1,), (0,)), ((), ()))
MESH = pl.DeviceIdType.MESH
TILE = 256


def iota(shape, dim):
    return lax.broadcasted_iota(jnp.int32, shape, dim)


def slot(row):
    return row - 4 if row >= 4 else row + 12


def slot_x(row):
    return row - 4 if row >= 4 else (row + 11 if row else 15)


def dense_taps(cell, frac, scale, out, tile, place, exact=False):
    u = cell.astype(F32) + (frac - 4.0)
    up = jnp.exp(u * INV)
    down = jnp.exp(u * (-INV))
    mid = jnp.exp(u * u * (-0.5 * INV)) * scale
    r = place(8)
    out[tile, 8 * r : 8 * r + 8, :] = mid
    below = [cell <= j for j in range(7)]
    p, q = mid, mid
    for k in range(1, 8):
        step = math.exp(-(2 * k - 1) * 0.5 * INV)
        p = p * (up * step) if exact else p * up
        q = q * (down * step) if exact else q * down
        r = place(8 + k)
        out[tile, 8 * r : 8 * r + 8, :] = jnp.where(below[k - 1], 0.0, p)
        r = place(8 - k)
        out[tile, 8 * r : 8 * r + 8, :] = jnp.where(below[7 - k], q, 0.0)


def crossed(x, y, tile, b):
    yy = y[tile, pl.ds(b, 16, stride=8), :].astype(BF16)
    parts = []
    for a in range(15):
        x8 = x[tile, pl.ds(a * 8 + b, 8, stride=0), :]
        parts.append(jnp.concatenate([x8, x8], 0).astype(BF16) * yy)
    return jnp.concatenate(parts + [jnp.zeros((16, 128), BF16)], 0)


def sincos(q, extent):
    eighth = extent // 8
    s = q + eighth
    quad = (s >> (extent.bit_length() - 3)) & 3
    r = ((s & (2 * eighth - 1)) - eighth).astype(F32) * (2.0 * math.pi / extent)
    r2 = r * r
    sin = r * (1.0 + r2 * (-1 / 6 + r2 * (1 / 120 + r2 * (-1 / 5040 + r2 * (1 / 362880)))))
    cos = 1.0 + r2 * (-0.5 + r2 * (1 / 24 + r2 * (-1 / 720 + r2 * (1 / 40320 + r2 * (-1 / 3628800)))))
    odd = (quad & 1) == 1
    c = jnp.where(odd, sin, cos)
    s = jnp.where(odd, cos, sin)
    c = jnp.where((quad == 1) | (quad == 2), -c, c)
    s = jnp.where(quad >= 2, -s, s)
    return c, s


def split(v):
    hi = v.astype(BF16)
    return hi, (v - hi.astype(F32)).astype(BF16)


def mm(a, b, dims=NN):
    return lax.dot_general(a, b, dims, preferred_element_type=F32)


def fused_kernel(
    cnt, cell_in, frac_in, w_in, mh, mk, ml,
    dens, inten,
    cell, frac, w, in_sem,
    packed, fx, fy, fz, ws, xa, ya, za, xb, yb, zb, side_a, side_b, inner, edge, tab_hi, tab_lo, zsum, tt, d_hi, d_lo,
    amps, q, up_buf, down_buf, up_got, down_got, right_got, left_got, got1, part, got2,
    s1, g1, s2, g2, up_s, up_g, down_s, down_g, right_s, right_g, left_s, left_g,
):
    nx, ny = lax.axis_size("gx"), lax.axis_size("gy")
    me_x, me_y = lax.axis_index("gx"), lax.axis_index("gy")
    remote = nx > 1
    loads = [pltpu.make_async_copy(cell_in, cell, in_sem.at[0])]
    loads += [pltpu.make_async_copy(frac_in.at[d], frac.at[d], in_sem.at[1 + d]) for d in range(3)]
    loads += [pltpu.make_async_copy(w_in, w, in_sem.at[4])]
    for load in loads:
        load.start()
    if remote:
        barrier = pltpu.get_barrier_semaphore()

        def greet_y(d, _):
            pl.semaphore_signal(barrier, inc=1, device_id=(me_x, (me_y + d) % ny), device_id_type=MESH)
            return 0

        def greet_x(d, _):
            pl.semaphore_signal(barrier, inc=1, device_id=((me_x + d) % nx, me_y), device_id_type=MESH)
            return 0

        lax.fori_loop(1, ny, greet_y, 0)
        lax.fori_loop(1, nx, greet_x, 0)

    def first(d, v):
        to = (me_y + d) % ny
        two = pl.ds(2 * v, 2)
        return pltpu.make_async_remote_copy(
            amps.at[to, two], got1.at[d, two], s1.at[v, d], g1.at[v, d], device_id=(me_x, to), device_id_type=MESH
        )

    def second(d):
        to = (me_x + d) % nx
        return pltpu.make_async_remote_copy(
            part.at[to // 2], got2.at[d], s2.at[d], g2.at[d], device_id=(to, me_y), device_id_type=MESH
        )

    def piece(src, dst, ss, gs, t, to):
        z = pl.ds(pl.multiple_of(t * TILE, TILE), TILE)
        return pltpu.make_async_remote_copy(
            src.at[:, :, z], dst.at[:, :, z], ss.at[t], gs.at[t], device_id=to, device_id_type=MESH
        )

    def ups(t):
        return piece(up_buf, up_got, up_s, up_g, t, (me_x, (me_y + 1) % ny))

    def downs(t):
        return piece(down_buf, down_got, down_s, down_g, t, (me_x, (me_y + ny - 1) % ny))

    def rights(t):
        return piece(q.at[pl.ds(8, 4)], right_got, right_s, right_g, t, ((me_x + 1) % nx, me_y))

    def lefts(t):
        return piece(q.at[pl.ds(12, 3)], left_got, left_s, left_g, t, ((me_x + nx - 1) % nx, me_y))

    row8 = iota((8, 128), 0)
    lcol = jnp.concatenate([ml[v // 2] + (row8 + 8 * (v % 2) - 8) for v in range(16)], 0)
    c0, s0 = sincos((lcol * iota((128, 128), 1)) & 1023, 1024)
    cw, sw = sincos((lcol * 128) & 1023, 1024)
    for t in range(8):
        for half, v in ((0, c0), (1, -s0)):
            hi, lo = split(v)
            tab_hi[128 * half : 128 * half + 128, 128 * t : 128 * t + 128] = hi
            tab_lo[128 * half : 128 * half + 128, 128 * t : 128 * t + 128] = lo
        c0, s0 = c0 * cw - s0 * sw, s0 * cw + c0 * sw
    zsum[...] = jnp.zeros_like(zsum)

    for o in (ya, za, yb, zb):
        for t in range(9):
            o[t, 96:104, :] = jnp.zeros((8, 128), F32)

    def pieces(fn, out):
        for t in range(9):
            if t < 8:
                v = fn(t // 4, 128 * (t % 4), 128)
            else:
                v = jnp.concatenate([fn(0, 512, 64), fn(1, 512, 64)], 0)
            out[t] = v.T

    loads[0].wait()
    pieces(lambda c, s, n: cell[0, c, s : s + n] + cell[1, c, s : s + n] * 8 + cell[2, c, s : s + n] * 64, packed)
    for d, o in ((0, fx), (1, fy), (2, fz)):
        loads[1 + d].wait()
        pieces(lambda c, s, n: frac[d, c, s : s + n], o)

    def weigh(c, s, n):
        taken = iota((n, 128), 0) + s < cnt[c : c + 1, :]
        return jnp.where(taken, w[c, s : s + n] * NORMAL, 0.0)

    loads[4].wait()
    pieces(weigh, ws)
    x0 = me_x * 8
    y0 = me_y * 16
    n = iota((16, 256), 1)
    ip = (n & 63) >> 2
    ni = (ip & 1) * 8 + (ip >> 1) - 8
    nj = (n >> 6) * 4 + (n & 3) - 8
    off = iota((16, 256), 0)
    off_x = jnp.where(off < 12, off, off - 15)
    off_y = jnp.where(off < 12, off, off - 16)

    def dense(g, t, taps):
        gs = pl.ds(pl.multiple_of(g * 8, 8), 8)
        p = packed[t, gs, :]
        dense_taps(p & 7, fx[t, gs, :], 1.0, taps[0], t, slot_x)
        dense_taps((p >> 3) & 7, fy[t, gs, :], 1.0, taps[1], t, slot)
        dense_taps(p >> 6, fz[t, gs, :], ws[t, gs, :], taps[2], t, slot, exact=True)

    lane16 = iota((16, 128), 1)

    def group(g, taps, side):
        xs, ys, zs = taps
        for t in range(9):
            dense(g, t, taps)

        def wide(ts, b):
            zz = jnp.concatenate([zs[t, pl.ds(b, 16, stride=8), :] for t in ts], 1).astype(BF16)
            return zz, jnp.concatenate([crossed(xs, ys, t, b) for t in ts], 1)

        for b in range(8):
            base = pl.multiple_of(g * 64 + b * 8, 8)
            here, there = pl.ds(base, 8), pl.ds(base + 8, 8)
            zt = zs[8, pl.ds(b, 16, stride=8), :]
            zm = jnp.concatenate([jnp.where(lane16 < 64, zt, 0.0), jnp.where(lane16 < 64, 0.0, zt)], 0)
            zz, cc = wide((4, 5), b)
            st = mm(cc, zz, NT)
            fm = mm(zm.astype(BF16), crossed(xs, ys, 8, b), NT)
            zz, cc = wide((0, 1), b)
            f = fm[0:16] + mm(zz, cc, NT)
            zz, cc = wide((6, 7), b)
            st = st + mm(cc, zz, NT)
            zz, cc = wide((2, 3), b)
            f = f + mm(zz, cc, NT)
            side[:, 16 * b : 16 * b + 16] = st
            inner[0, here, :] = f[0:8]
            edge[0, there, :] = f[8:16]
            inner[1, here, :] = fm[16:24]
            edge[1, there, :] = fm[24:32]

        tr = side[...].T
        for b in range(8):
            base = pl.multiple_of(g * 64 + b * 8, 8)
            inner[1, pl.ds(base, 8), :] += tr[16 * b : 16 * b + 8]
            edge[1, pl.ds(base + 8, 8), :] += tr[16 * b + 8 : 16 * b + 16]

    taps_a, taps_b = (xa, ya, za), (xb, yb, zb)

    def groups(i, _):
        group((2 * i + 15) & 15, taps_a, side_a)
        group((2 * i) & 15, taps_b, side_b)
        return 0

    low256 = (iota((TILE, 256), 0) & 7) < 4
    lane = iota((8, 256), 1)
    k2 = jnp.zeros((8, 256), F32)
    for row in range(1, 16):
        square = float((row - 8) ** 2)
        k2 = k2 + jnp.where((lane >> 4) == slot_x(row), square, 0.0) + jnp.where((lane & 15) == slot(row), square, 0.0)
    gain = jnp.exp(k2 * (-0.5 * INV)) * (NORMAL * NORMAL)
    low = iota((8, TILE), 0) < 4

    def density_tile(t):
        z0 = pl.multiple_of(t * TILE, TILE)
        z = pl.ds(z0, TILE)
        spread = lambda v: jnp.concatenate([v] * (TILE // 8), 0)
        for c in range(2):
            beyond = jnp.where(low256, edge[c, z, :], edge[c, pl.ds(z0 + 16, TILE), :])
            d = (inner[c, z, :] + beyond) * spread(gain)
            tt[c] = d.T
            hi, lo = split(d)
            d_hi[...] = hi
            d_lo[...] = lo
            th = tab_hi[:, z]
            tl = tab_lo[:, z]
            zsum[c] += mm(th, d_hi[...]) + mm(th, d_lo[...]) + mm(tl, d_hi[...])

    def assemble(t):
        z = pl.ds(pl.multiple_of(t * TILE, TILE), TILE)
        for k in range(8):
            tops, bottoms = [], []
            for a in (2 * k, 2 * k + 1):
                in0, out0 = tt[0, 16 * a : 16 * a + 8, :], tt[0, 16 * a + 8 : 16 * a + 16, :]
                in1, out1 = tt[1, 16 * a : 16 * a + 8, :], tt[1, 16 * a + 8 : 16 * a + 16, :]
                q[a, 0:8, z] = in0 + jnp.where(low, 0.0, out1)
                q[a, 8:16, z] = in1 + jnp.where(low, out0, 0.0)
                tops.append(out1)
                bottoms.append(out0)
            up_buf[k, :, z] = jnp.where(low, tops[0], pltpu.roll(tops[1], 4, 0))
            down_buf[k, :, z] = jnp.where(low, pltpu.roll(bottoms[0], 4, 0), bottoms[1])

    def fold_y(t):
        z = pl.ds(pl.multiple_of(t * TILE, TILE), TILE)
        for k in (4, 5, 6, 7, 0, 1, 2, 3):
            a = 2 * k
            u, d = up_got[k, :, z], down_got[k, :, z]
            q[a, 0:8, z] += jnp.where(low, u, 0.0)
            q[a + 1, 0:8, z] += jnp.where(low, pltpu.roll(u, 4, 0), 0.0)
            q[a, 8:16, z] += jnp.where(low, 0.0, pltpu.roll(d, 4, 0))
            q[a + 1, 8:16, z] += jnp.where(low, 0.0, d)

    def pass_on(t):
        if remote:
            ups(t).wait()
            downs(t).wait()
        fold_y(t)
        if remote:
            rights(t).start()
            lefts(t).start()

    def tiles(t, _):
        lax.fori_loop(jnp.where(t == 0, 0, 2 * t + 1), jnp.where(t == 3, 8, 2 * t + 3), groups, 0)

        @pl.when(t == 0)
        def _():
            for c in range(2):
                edge[c, 0:8, :] = edge[c, 1024:1032, :]

        @pl.when(t == 3)
        def _():
            for c in range(2):
                edge[c, 1032:1040, :] = edge[c, 8:16, :]

        density_tile(t)

        @pl.when(t < 3)
        def _():
            assemble(t)
            if remote:

                @pl.when(t == 0)
                def _():
                    pl.semaphore_wait(barrier, nx + ny - 2)

                ups(t).start()
                downs(t).start()

            @pl.when(t > 0)
            def _():
                pass_on(t - 1)

        return 0

    lax.fori_loop(0, 4, tiles, 0)

    lane_low = iota((16, 128), 1) < 64

    def pair(v, _):
        us = []
        for e in range(2):
            win = 2 * v + e
            pr, pi = sincos(((mk[win] + nj[0:1]) * 8) & 127, 128)
            xr, xi = sincos(((mh[win] + ni) * (x0 + off_x)) & 127, 128)
            yr, yi = sincos(((mk[win] + nj) * (y0 + off_y)) & 127, 128)
            mr, mi = [], []
            for a in range(16):
                mr.append(xr[a : a + 1] * yr - xi[a : a + 1] * yi)
                mi.append(-(xr[a : a + 1] * yi + xi[a : a + 1] * yr))
            mrh, mrl = split(jnp.concatenate(mr, 0))
            mih, mil = split(jnp.concatenate(mi, 0))
            rows = [
                zsum[c, pl.ds(pl.multiple_of(128 * half + win * 16, 16), 16), :] for c in (0, 1) for half in (0, 1)
            ]
            zh, zl = split(jnp.concatenate(rows, 0))
            A = mm(zh, mrh) + mm(zl, mrh) + mm(zh, mrl)
            B = mm(zh, mih) + mm(zl, mih) + mm(zh, mil)
            re0, im0 = A[0:16] - B[16:32], A[16:32] + B[0:16]
            re1, im1 = A[32:48] - B[48:64], A[48:64] + B[32:48]
            us.append((re0 + re1 * pr + im1 * pi, im0 + im1 * pr - re1 * pi))
        rows = []
        for jh in range(4):
            for half in range(2):
                a0 = us[0][half][:, 128 * (jh // 2) : 128 * (jh // 2) + 128]
                a1 = us[1][half][:, 128 * (jh // 2) : 128 * (jh // 2) + 128]
                if jh % 2 == 0:
                    rows.append(jnp.where(lane_low, a0, pltpu.roll(a1, 64, 1)))
                else:
                    rows.append(jnp.where(lane_low, pltpu.roll(a0, 64, 1), a1))
        tr = jnp.concatenate(rows, 0).T
        for e in range(2):
            for il in range(8):
                amps[il, 2 * v + e] = tr[64 * e + 8 * il : 64 * e + 8 * il + 8]
        if remote:

            def send(d, _):
                first(d, v).start()
                return 0

            lax.fori_loop(1, ny, send, 0)
        return 0

    lax.fori_loop(0, 4, pair, 0)
    assemble(3)
    if remote:
        ups(3).start()
        downs(3).start()
    pass_on(2)

    if not remote:
        pass_on(3)
        dens[...] = q[0:8]
        inten[...] = amps[0, 0]
        return

    def finish_first(i, _):
        first(1 + i // 4, i % 4).wait()
        return 0

    lax.fori_loop(0, 4 * (ny - 1), finish_first, 0)
    own = amps[me_y]
    for d in range(1, 8):
        own = own + got1[d]
    part[...] = own

    def send_second(d, _):
        second(d).start()
        return 0

    def finish_second(d, _):
        second(d).wait()
        return 0

    lax.fori_loop(1, nx, send_second, 0)
    odd = (iota((8, 128), 0) * 0 + me_x % 2) == 1
    pass_on(3)
    lax.fori_loop(1, nx, finish_second, 0)
    total = part[me_x // 2]
    for d in range(1, 16):
        total = total + got2[d]
    mine = jnp.where(odd, pltpu.roll(total, 4, 0), total)
    power = mine * mine
    power = power + pltpu.roll(power, 112, 1)
    inten[...] = power

    for t in range(4):
        z = slice(t * TILE, t * TILE + TILE)
        rights(t).wait()
        lefts(t).wait()
        dens[0:4, :, z] = q[0:4, :, z] + right_got[:, :, z]
        dens[4:5, :, z] = q[4:5, :, z]
        dens[5:8, :, z] = q[5:8, :, z] + left_got[:, :, z]


def local(cell, frac, w, cnt, mh, mk, ml):
    cell = jnp.swapaxes(cell, 2, 3)
    frac = jnp.swapaxes(frac, 2, 3)
    w = jnp.swapaxes(w, 1, 2)
    vm = pl.BlockSpec(memory_space=pltpu.VMEM)
    sm = pl.BlockSpec(memory_space=pltpu.SMEM)
    hbm = pl.BlockSpec(memory_space=pltpu.HBM)
    sd = jax.ShapeDtypeStruct
    vmem = pltpu.VMEM
    dma = pltpu.SemaphoreType.DMA
    multi = lax.axis_size("gx") > 1
    return pl.pallas_call(
        fused_kernel,
        out_shape=(sd((8, 16, 1024), F32), sd((8, 128), F32)),
        in_specs=[vm] + [hbm] * 3 + [sm] * 3,
        out_specs=(vm, vm),
        scratch_shapes=[
            vmem((3, 2, 576, 128), jnp.int32),
            vmem((3, 2, 576, 128), F32),
            vmem((2, 576, 128), F32),
            dma((5,)),
            vmem((9, 128, 128), jnp.int32),
        ]
        + [vmem((9, 128, 128), F32)] * 10
        + [
            vmem((256, 128), F32),
            vmem((256, 128), F32),
            vmem((2, 1024, 256), F32),
            vmem((2, 1040, 256), F32),
            vmem((256, 1024), BF16),
            vmem((256, 1024), BF16),
            vmem((2, 256, 256), F32),
            vmem((2, 256, TILE), F32),
            vmem((TILE, 256), BF16),
            vmem((TILE, 256), BF16),
            vmem((8, 8, 8, 128), F32),
            vmem((16, 16, 1024), F32),
            vmem((8, 8, 1024), F32),
            vmem((8, 8, 1024), F32),
            vmem((8, 8, 1024), F32),
            vmem((8, 8, 1024), F32),
            vmem((4, 16, 1024), F32),
            vmem((3, 16, 1024), F32),
            vmem((8, 8, 8, 128), F32),
            vmem((8, 8, 128), F32),
            vmem((16, 8, 128), F32),
            dma((4, 8)), dma((4, 8)), dma((16,)), dma((16,)),
        ]
        + [dma((4,))] * 8,
        compiler_params=pltpu.CompilerParams(
            collective_id=0 if multi else None, has_side_effects=True,
            vmem_limit_bytes=58 * 2**20
        ),
    )(cnt, cell, frac, w, mh, mk, ml)


def output_kernel(density, power, dens, inten):
    dens[...] = density[...]
    n = iota((128, 256), 1)
    pick = (iota((128, 256), 0) == (n >> 6) * 32 + (n & 15)).astype(F32)
    wide = lax.dot_general(power[...], pick, NN, precision=lax.Precision.HIGHEST, preferred_element_type=F32)
    keep = iota((8, 256), 0) == ((iota((8, 256), 1) >> 4) & 3)
    inten[...] = jnp.sum(jnp.where(keep, wide, 0.0), axis=0, keepdims=True) * (1.0 / 16777216.0)


def outputs(density, power):
    vm = pl.BlockSpec(memory_space=pltpu.VMEM)
    return pl.pallas_call(
        output_kernel,
        out_shape=(jax.ShapeDtypeStruct((8, 16, 1024), F32), jax.ShapeDtypeStruct((1, 256), F32)),
        in_specs=[vm, vm],
        out_specs=(vm, vm),
        compiler_params=pltpu.CompilerParams(vmem_limit_bytes=58 * 2**20),
    )(density, power)


def shards(atom_cell, atom_frac, atom_weight, block_count, miller_h, miller_k, miller_l):
    return outputs(
        *local(atom_cell[:, 0], atom_frac[:, 0], atom_weight[0], block_count[0], miller_h, miller_k, miller_l)
    )


def solution(mesh):
    in_specs = (
        P(None, "gx", "gy", None, None),
        P(None, "gx", "gy", None, None),
        P("gx", "gy", None, None),
        P("gx", "gy", None),
        P(),
        P(),
        P(),
    )
    out_specs = (P("gx", "gy", None), P(("gx", "gy"), None))
    return jax.shard_map(shards, mesh=mesh, in_specs=in_specs, out_specs=out_specs, check_vma=False)
```

```python
import math

import jax
import jax.numpy as jnp
from jax import lax
from jax.experimental import pallas as pl
from jax.experimental.pallas import tpu as pltpu
from jax.sharding import PartitionSpec as P

SIGMA2 = 0.9 * 0.9
INV = 1.0 / SIGMA2
NORMAL = 1.0 / (0.9 * math.sqrt(2.0 * math.pi))
F32 = jnp.float32
BF16 = jnp.bfloat16
NT = (((1,), (1,)), ((), ()))
NN = (((1,), (0,)), ((), ()))
MESH = pl.DeviceIdType.MESH
TILE = 256


def iota(shape, dim):
    return lax.broadcasted_iota(jnp.int32, shape, dim)


def slot(row):
    return row - 4 if row >= 4 else row + 12


def slot_x(row):
    return row - 4 if row >= 4 else (row + 11 if row else 15)


def dense_taps(cell, frac, scale, out, tile, place, exact=False):
    u = cell.astype(F32) + (frac - 4.0)
    up = jnp.exp(u * INV)
    down = jnp.exp(u * (-INV))
    mid = jnp.exp(u * u * (-0.5 * INV)) * scale
    r = place(8)
    out[tile, 8 * r : 8 * r + 8, :] = mid
    below = [cell <= j for j in range(7)]
    p, q = mid, mid
    for k in range(1, 8):
        step = math.exp(-(2 * k - 1) * 0.5 * INV)
        p = p * (up * step) if exact else p * up
        q = q * (down * step) if exact else q * down
        r = place(8 + k)
        out[tile, 8 * r : 8 * r + 8, :] = jnp.where(below[k - 1], 0.0, p)
        r = place(8 - k)
        out[tile, 8 * r : 8 * r + 8, :] = jnp.where(below[7 - k], q, 0.0)


def crossed(x, y, tile, b):
    yy = y[tile, pl.ds(b, 16, stride=8), :].astype(BF16)
    parts = []
    for a in range(15):
        x8 = x[tile, pl.ds(a * 8 + b, 8, stride=0), :]
        parts.append(jnp.concatenate([x8, x8], 0).astype(BF16) * yy)
    return jnp.concatenate(parts + [jnp.zeros((16, 128), BF16)], 0)


def sincos(q, extent):
    eighth = extent // 8
    s = q + eighth
    quad = (s >> (extent.bit_length() - 3)) & 3
    r = ((s & (2 * eighth - 1)) - eighth).astype(F32) * (2.0 * math.pi / extent)
    r2 = r * r
    sin = r * (1.0 + r2 * (-1 / 6 + r2 * (1 / 120 + r2 * (-1 / 5040 + r2 * (1 / 362880)))))
    cos = 1.0 + r2 * (-0.5 + r2 * (1 / 24 + r2 * (-1 / 720 + r2 * (1 / 40320 + r2 * (-1 / 3628800)))))
    odd = (quad & 1) == 1
    c = jnp.where(odd, sin, cos)
    s = jnp.where(odd, cos, sin)
    c = jnp.where((quad == 1) | (quad == 2), -c, c)
    s = jnp.where(quad >= 2, -s, s)
    return c, s


def split(v):
    hi = v.astype(BF16)
    return hi, (v - hi.astype(F32)).astype(BF16)


def mm(a, b, dims=NN):
    return lax.dot_general(a, b, dims, preferred_element_type=F32)


def fused_kernel(
    cnt, cell_in, frac_in, w_in, mh, mk, ml,
    dens, inten,
    cell, frac, w, in_sem,
    packed, fx, fy, fz, ws, xa, ya, za, xb, yb, zb, side_a, side_b, inner, edge, tab_hi, tab_lo, zsum, tt, d_hi, d_lo,
    amps, q, up_buf, down_buf, up_got, down_got, right_got, left_got, got1, part, got2,
    s1, g1, s2, g2, up_s, up_g, down_s, down_g, right_s, right_g, left_s, left_g,
):
    nx, ny = lax.axis_size("gx"), lax.axis_size("gy")
    me_x, me_y = lax.axis_index("gx"), lax.axis_index("gy")
    remote = nx > 1
    loads = [pltpu.make_async_copy(cell_in, cell, in_sem.at[0])]
    loads += [pltpu.make_async_copy(frac_in.at[d], frac.at[d], in_sem.at[1 + d]) for d in range(3)]
    loads += [pltpu.make_async_copy(w_in, w, in_sem.at[4])]
    for load in loads:
        load.start()
    if remote:
        barrier = pltpu.get_barrier_semaphore()

        def greet_y(d, _):
            pl.semaphore_signal(barrier, inc=1, device_id=(me_x, (me_y + d) % ny), device_id_type=MESH)
            return 0

        def greet_x(d, _):
            pl.semaphore_signal(barrier, inc=1, device_id=((me_x + d) % nx, me_y), device_id_type=MESH)
            return 0

        for d in range(1, ny):
            greet_y(d, 0)
        for d in range(1, nx):
            greet_x(d, 0)

    def first(d, v):
        to = (me_y + d) % ny
        two = pl.ds(2 * v, 2)
        return pltpu.make_async_remote_copy(
            amps.at[to, two], got1.at[d, two], s1.at[v, d], g1.at[v, d], device_id=(me_x, to), device_id_type=MESH
        )

    def second(d):
        to = (me_x + d) % nx
        return pltpu.make_async_remote_copy(
            part.at[to // 2], got2.at[d], s2.at[d], g2.at[d], device_id=(to, me_y), device_id_type=MESH
        )

    def piece(src, dst, ss, gs, t, to):
        z = pl.ds(pl.multiple_of(t * TILE, TILE), TILE)
        return pltpu.make_async_remote_copy(
            src.at[:, :, z], dst.at[:, :, z], ss.at[t], gs.at[t], device_id=to, device_id_type=MESH
        )

    def ups(t):
        return piece(up_buf, up_got, up_s, up_g, t, (me_x, (me_y + 1) % ny))

    def downs(t):
        return piece(down_buf, down_got, down_s, down_g, t, (me_x, (me_y + ny - 1) % ny))

    def rights(t):
        return piece(q.at[pl.ds(8, 4)], right_got, right_s, right_g, t, ((me_x + 1) % nx, me_y))

    def lefts(t):
        return piece(q.at[pl.ds(12, 3)], left_got, left_s, left_g, t, ((me_x + nx - 1) % nx, me_y))

    row8 = iota((8, 128), 0)
    lcol = jnp.concatenate([ml[v // 2] + (row8 + 8 * (v % 2) - 8) for v in range(16)], 0)
    c0, s0 = sincos((lcol * iota((128, 128), 1)) & 1023, 1024)
    cw, sw = sincos((lcol * 128) & 1023, 1024)
    for t in range(8):
        for half, v in ((0, c0), (1, -s0)):
            hi, lo = split(v)
            tab_hi[128 * half : 128 * half + 128, 128 * t : 128 * t + 128] = hi
            tab_lo[128 * half : 128 * half + 128, 128 * t : 128 * t + 128] = lo
        c0, s0 = c0 * cw - s0 * sw, s0 * cw + c0 * sw
    zsum[...] = jnp.zeros_like(zsum)

    for o in (ya, za, yb, zb):
        for t in range(9):
            o[t, 96:104, :] = jnp.zeros((8, 128), F32)

    def pieces(fn, out):
        for t in range(9):
            if t < 8:
                v = fn(t // 4, 128 * (t % 4), 128)
            else:
                v = jnp.concatenate([fn(0, 512, 64), fn(1, 512, 64)], 0)
            out[t] = v.T

    loads[0].wait()
    pieces(lambda c, s, n: cell[0, c, s : s + n] + cell[1, c, s : s + n] * 8 + cell[2, c, s : s + n] * 64, packed)
    for d, o in ((0, fx), (1, fy), (2, fz)):
        loads[1 + d].wait()
        pieces(lambda c, s, n: frac[d, c, s : s + n], o)

    def weigh(c, s, n):
        taken = iota((n, 128), 0) + s < cnt[c : c + 1, :]
        return jnp.where(taken, w[c, s : s + n] * NORMAL, 0.0)

    loads[4].wait()
    pieces(weigh, ws)
    x0 = me_x * 8
    y0 = me_y * 16
    n = iota((16, 256), 1)
    ip = (n & 63) >> 2
    ni = (ip & 1) * 8 + (ip >> 1) - 8
    nj = (n >> 6) * 4 + (n & 3) - 8
    off = iota((16, 256), 0)
    off_x = jnp.where(off < 12, off, off - 15)
    off_y = jnp.where(off < 12, off, off - 16)

    def dense(g, t, taps):
        gs = pl.ds(pl.multiple_of(g * 8, 8), 8)
        p = packed[t, gs, :]
        dense_taps(p & 7, fx[t, gs, :], 1.0, taps[0], t, slot_x)
        dense_taps((p >> 3) & 7, fy[t, gs, :], 1.0, taps[1], t, slot)
        dense_taps(p >> 6, fz[t, gs, :], ws[t, gs, :], taps[2], t, slot, exact=True)

    lane16 = iota((16, 128), 1)

    def group(g, taps, side):
        xs, ys, zs = taps
        for t in range(9):
            dense(g, t, taps)

        def wide(ts, b):
            zz = jnp.concatenate([zs[t, pl.ds(b, 16, stride=8), :] for t in ts], 1).astype(BF16)
            return zz, jnp.concatenate([crossed(xs, ys, t, b) for t in ts], 1)

        for b in range(8):
            base = pl.multiple_of(g * 64 + b * 8, 8)
            here, there = pl.ds(base, 8), pl.ds(base + 8, 8)
            zt = zs[8, pl.ds(b, 16, stride=8), :]
            zm = jnp.concatenate([jnp.where(lane16 < 64, zt, 0.0), jnp.where(lane16 < 64, 0.0, zt)], 0)
            zz, cc = wide((4, 5), b)
            st = mm(cc, zz, NT)
            fm = mm(zm.astype(BF16), crossed(xs, ys, 8, b), NT)
            zz, cc = wide((0, 1), b)
            f = fm[0:16] + mm(zz, cc, NT)
            zz, cc = wide((6, 7), b)
            st = st + mm(cc, zz, NT)
            zz, cc = wide((2, 3), b)
            f = f + mm(zz, cc, NT)
            side[:, 16 * b : 16 * b + 16] = st
            inner[0, here, :] = f[0:8]
            edge[0, there, :] = f[8:16]
            inner[1, here, :] = fm[16:24]
            edge[1, there, :] = fm[24:32]

        tr = side[...].T
        for b in range(8):
            base = pl.multiple_of(g * 64 + b * 8, 8)
            inner[1, pl.ds(base, 8), :] += tr[16 * b : 16 * b + 8]
            edge[1, pl.ds(base + 8, 8), :] += tr[16 * b + 8 : 16 * b + 16]

    taps_a, taps_b = (xa, ya, za), (xb, yb, zb)

    def groups(i, _):
        group((2 * i + 15) & 15, taps_a, side_a)
        group((2 * i) & 15, taps_b, side_b)
        return 0

    low256 = (iota((TILE, 256), 0) & 7) < 4
    lane = iota((8, 256), 1)
    k2 = jnp.zeros((8, 256), F32)
    for row in range(1, 16):
        square = float((row - 8) ** 2)
        k2 = k2 + jnp.where((lane >> 4) == slot_x(row), square, 0.0) + jnp.where((lane & 15) == slot(row), square, 0.0)
    gain = jnp.exp(k2 * (-0.5 * INV)) * (NORMAL * NORMAL)
    low = iota((8, TILE), 0) < 4

    def density_tile(t):
        z0 = pl.multiple_of(t * TILE, TILE)
        z = pl.ds(z0, TILE)
        spread = lambda v: jnp.concatenate([v] * (TILE // 8), 0)
        for c in range(2):
            beyond = jnp.where(low256, edge[c, z, :], edge[c, pl.ds(z0 + 16, TILE), :])
            d = (inner[c, z, :] + beyond) * spread(gain)
            tt[c] = d.T
            hi, lo = split(d)
            d_hi[...] = hi
            d_lo[...] = lo
            th = tab_hi[:, z]
            tl = tab_lo[:, z]
            zsum[c] += mm(th, d_hi[...]) + mm(th, d_lo[...]) + mm(tl, d_hi[...])

    def assemble(t):
        z = pl.ds(pl.multiple_of(t * TILE, TILE), TILE)
        for k in range(8):
            tops, bottoms = [], []
            for a in (2 * k, 2 * k + 1):
                in0, out0 = tt[0, 16 * a : 16 * a + 8, :], tt[0, 16 * a + 8 : 16 * a + 16, :]
                in1, out1 = tt[1, 16 * a : 16 * a + 8, :], tt[1, 16 * a + 8 : 16 * a + 16, :]
                q[a, 0:8, z] = in0 + jnp.where(low, 0.0, out1)
                q[a, 8:16, z] = in1 + jnp.where(low, out0, 0.0)
                tops.append(out1)
                bottoms.append(out0)
            up_buf[k, :, z] = jnp.where(low, tops[0], pltpu.roll(tops[1], 4, 0))
            down_buf[k, :, z] = jnp.where(low, pltpu.roll(bottoms[0], 4, 0), bottoms[1])

    def fold_y(t):
        z = pl.ds(pl.multiple_of(t * TILE, TILE), TILE)
        for k in (4, 5, 6, 7, 0, 1, 2, 3):
            a = 2 * k
            u, d = up_got[k, :, z], down_got[k, :, z]
            q[a, 0:8, z] += jnp.where(low, u, 0.0)
            q[a + 1, 0:8, z] += jnp.where(low, pltpu.roll(u, 4, 0), 0.0)
            q[a, 8:16, z] += jnp.where(low, 0.0, pltpu.roll(d, 4, 0))
            q[a + 1, 8:16, z] += jnp.where(low, 0.0, d)

    def pass_on(t):
        if remote:
            ups(t).wait()
            downs(t).wait()
        fold_y(t)
        if remote:
            rights(t).start()
            lefts(t).start()

    def tiles(t, _):
        lax.fori_loop(jnp.where(t == 0, 0, 2 * t + 1), jnp.where(t == 3, 8, 2 * t + 3), groups, 0)

        @pl.when(t == 0)
        def _():
            for c in range(2):
                edge[c, 0:8, :] = edge[c, 1024:1032, :]

        @pl.when(t == 3)
        def _():
            for c in range(2):
                edge[c, 1032:1040, :] = edge[c, 8:16, :]

        density_tile(t)

        @pl.when(t < 3)
        def _():
            assemble(t)
            if remote:

                @pl.when(t == 0)
                def _():
                    pl.semaphore_wait(barrier, nx + ny - 2)

                ups(t).start()
                downs(t).start()

            @pl.when(t > 0)
            def _():
                pass_on(t - 1)

        return 0

    lax.fori_loop(0, 4, tiles, 0)

    lane_low = iota((16, 128), 1) < 64

    def pair(v, _):
        us = []
        for e in range(2):
            win = 2 * v + e
            pr, pi = sincos(((mk[win] + nj[0:1]) * 8) & 127, 128)
            xr, xi = sincos(((mh[win] + ni) * (x0 + off_x)) & 127, 128)
            yr, yi = sincos(((mk[win] + nj) * (y0 + off_y)) & 127, 128)
            mr, mi = [], []
            for a in range(16):
                mr.append(xr[a : a + 1] * yr - xi[a : a + 1] * yi)
                mi.append(-(xr[a : a + 1] * yi + xi[a : a + 1] * yr))
            mrh, mrl = split(jnp.concatenate(mr, 0))
            mih, mil = split(jnp.concatenate(mi, 0))
            rows = [
                zsum[c, pl.ds(pl.multiple_of(128 * half + win * 16, 16), 16), :] for c in (0, 1) for half in (0, 1)
            ]
            zh, zl = split(jnp.concatenate(rows, 0))
            A = mm(zh, mrh) + mm(zl, mrh) + mm(zh, mrl)
            B = mm(zh, mih) + mm(zl, mih) + mm(zh, mil)
            re0, im0 = A[0:16] - B[16:32], A[16:32] + B[0:16]
            re1, im1 = A[32:48] - B[48:64], A[48:64] + B[32:48]
            us.append((re0 + re1 * pr + im1 * pi, im0 + im1 * pr - re1 * pi))
        rows = []
        for jh in range(4):
            for half in range(2):
                a0 = us[0][half][:, 128 * (jh // 2) : 128 * (jh // 2) + 128]
                a1 = us[1][half][:, 128 * (jh // 2) : 128 * (jh // 2) + 128]
                if jh % 2 == 0:
                    rows.append(jnp.where(lane_low, a0, pltpu.roll(a1, 64, 1)))
                else:
                    rows.append(jnp.where(lane_low, pltpu.roll(a0, 64, 1), a1))
        tr = jnp.concatenate(rows, 0).T
        for e in range(2):
            for il in range(8):
                amps[il, 2 * v + e] = tr[64 * e + 8 * il : 64 * e + 8 * il + 8]
        if remote:

            def send(d, _):
                first(d, v).start()
                return 0

            for d in range(1, ny):
                send(d, 0)
        return 0

    lax.fori_loop(0, 4, pair, 0)
    assemble(3)
    if remote:
        ups(3).start()
        downs(3).start()
    pass_on(2)

    if not remote:
        pass_on(3)
        dens[...] = q[0:8]
        inten[...] = amps[0, 0]
        return

    def finish_first(i, _):
        first(1 + i // 4, i % 4).wait()
        return 0

    for i in range(4 * (ny - 1)):
        finish_first(i, 0)
    own = amps[me_y]
    for d in range(1, 8):
        own = own + got1[d]
    part[...] = own

    def send_second(d, _):
        second(d).start()
        return 0

    def finish_second(d, _):
        second(d).wait()
        return 0

    for d in range(1, nx):
        send_second(d, 0)
    odd = (iota((8, 128), 0) * 0 + me_x % 2) == 1
    pass_on(3)
    for d in range(1, nx):
        finish_second(d, 0)
    total = part[me_x // 2]
    for d in range(1, 16):
        total = total + got2[d]
    mine = jnp.where(odd, pltpu.roll(total, 4, 0), total)
    power = mine * mine
    power = power + pltpu.roll(power, 112, 1)
    inten[...] = power

    for t in range(4):
        z = slice(t * TILE, t * TILE + TILE)
        rights(t).wait()
        lefts(t).wait()
        dens[0:4, :, z] = q[0:4, :, z] + right_got[:, :, z]
        dens[4:5, :, z] = q[4:5, :, z]
        dens[5:8, :, z] = q[5:8, :, z] + left_got[:, :, z]


def local(cell, frac, w, cnt, mh, mk, ml):
    cell = jnp.swapaxes(cell, 2, 3)
    frac = jnp.swapaxes(frac, 2, 3)
    w = jnp.swapaxes(w, 1, 2)
    vm = pl.BlockSpec(memory_space=pltpu.VMEM)
    sm = pl.BlockSpec(memory_space=pltpu.SMEM)
    hbm = pl.BlockSpec(memory_space=pltpu.HBM)
    sd = jax.ShapeDtypeStruct
    vmem = pltpu.VMEM
    dma = pltpu.SemaphoreType.DMA
    multi = lax.axis_size("gx") > 1
    return pl.pallas_call(
        fused_kernel,
        out_shape=(sd((8, 16, 1024), F32), sd((8, 128), F32)),
        in_specs=[vm] + [hbm] * 3 + [sm] * 3,
        out_specs=(vm, vm),
        scratch_shapes=[
            vmem((3, 2, 576, 128), jnp.int32),
            vmem((3, 2, 576, 128), F32),
            vmem((2, 576, 128), F32),
            dma((5,)),
            vmem((9, 128, 128), jnp.int32),
        ]
        + [vmem((9, 128, 128), F32)] * 10
        + [
            vmem((256, 128), F32),
            vmem((256, 128), F32),
            vmem((2, 1024, 256), F32),
            vmem((2, 1040, 256), F32),
            vmem((256, 1024), BF16),
            vmem((256, 1024), BF16),
            vmem((2, 256, 256), F32),
            vmem((2, 256, TILE), F32),
            vmem((TILE, 256), BF16),
            vmem((TILE, 256), BF16),
            vmem((8, 8, 8, 128), F32),
            vmem((16, 16, 1024), F32),
            vmem((8, 8, 1024), F32),
            vmem((8, 8, 1024), F32),
            vmem((8, 8, 1024), F32),
            vmem((8, 8, 1024), F32),
            vmem((4, 16, 1024), F32),
            vmem((3, 16, 1024), F32),
            vmem((8, 8, 8, 128), F32),
            vmem((8, 8, 128), F32),
            vmem((16, 8, 128), F32),
            dma((4, 8)), dma((4, 8)), dma((16,)), dma((16,)),
        ]
        + [dma((4,))] * 8,
        compiler_params=pltpu.CompilerParams(
            collective_id=0 if multi else None, has_side_effects=True,
            vmem_limit_bytes=58 * 2**20
        ),
    )(cnt, cell, frac, w, mh, mk, ml)


def output_kernel(density, power, dens, inten):
    dens[...] = density[...]
    n = iota((128, 256), 1)
    pick = (iota((128, 256), 0) == (n >> 6) * 32 + (n & 15)).astype(F32)
    wide = lax.dot_general(power[...], pick, NN, precision=lax.Precision.HIGHEST, preferred_element_type=F32)
    keep = iota((8, 256), 0) == ((iota((8, 256), 1) >> 4) & 3)
    inten[...] = jnp.sum(jnp.where(keep, wide, 0.0), axis=0, keepdims=True) * (1.0 / 16777216.0)


def outputs(density, power):
    vm = pl.BlockSpec(memory_space=pltpu.VMEM)
    return pl.pallas_call(
        output_kernel,
        out_shape=(jax.ShapeDtypeStruct((8, 16, 1024), F32), jax.ShapeDtypeStruct((1, 256), F32)),
        in_specs=[vm, vm],
        out_specs=(vm, vm),
        compiler_params=pltpu.CompilerParams(vmem_limit_bytes=58 * 2**20),
    )(density, power)


def shards(atom_cell, atom_frac, atom_weight, block_count, miller_h, miller_k, miller_l):
    return outputs(
        *local(atom_cell[:, 0], atom_frac[:, 0], atom_weight[0], block_count[0], miller_h, miller_k, miller_l)
    )


def solution(mesh):
    in_specs = (
        P(None, "gx", "gy", None, None),
        P(None, "gx", "gy", None, None),
        P("gx", "gy", None, None),
        P("gx", "gy", None),
        P(),
        P(),
        P(),
    )
    out_specs = (P("gx", "gy", None), P(("gx", "gy"), None))
    return jax.shard_map(shards, mesh=mesh, in_specs=in_specs, out_specs=out_specs, check_vma=False)
```
